32 devices in a mesh: grp: 2 (over y), seq: 4 (over z), section: 2 (over x), head: 2 (over core).
Axes of the slice: x: 2, y: 2, z: 4, core: 2. Of those that a mesh axis runs over, the one named last changes fastest.
Arguments:
- queries: bfloat16 [2048, 2048], P(('grp', 'seq'), ('section', 'head')), parts along dimension 0, may hold values from -6 to 6
- reflect_keys: bfloat16 [2048, 2, 2048], P(('grp', 'seq'), None, ('section', 'head')), parts along dimension 0, may hold values from -6 to 6
- reflect_values: bfloat16 [2048, 2, 2048], P(('grp', 'seq'), None, ('section', 'head')), parts along dimension 0, may hold values from -6 to 6
- reflect_betas: float32 [2048, 2, 16], P(('grp', 'seq'), None, ('section', 'head')), parts along dimension 0, may hold values from 0 to 2
- decay_rates: float32 [2048, 16], P(('grp', 'seq'), ('section', 'head')), parts along dimension 0, may hold values from 0 to 1
- resets: int32 [2048], P(('grp', 'seq')), parts along dimension 0, may hold values 0 or 1
- out_weight: bfloat16 [2048, 2048], P(('section', 'head')), may hold values from -0.125 to 0.125
- out_cotangent: bfloat16 [2048, 2048], P(('grp', 'seq'), ('section', 'head')), parts along dimension 0, may hold values from -6 to 6
Outputs:
- output_features: bfloat16 [2048, 2048], P(('section', 'head'), ('grp', 'seq')), parts along dimension 1
- value_grads: float32 [2048, 2, 2048], P(('grp', 'seq'), None, ('section', 'head')), parts along dimension 0
The draws below stay inside these ranges and needn't reach their ends.
There are 2 independent parts, one for each index of `grp`. The reference program is written for one: setup_inputs(seed, part) draws one part's arguments, and reference() takes and returns one part's arrays. A program takes and returns all parts, laid end to end along the dimension named above; an argument that names none is the same for every part. Nothing has to cross between parts.
Inputs may be any that keep to these rules, and one draw needn't show every extreme that they name: `resets`: 1 marks a token before which the state is cleared.
All inputs are finite; a program needn't handle non-finite values. No bound on the sum of `resets` on one device may be relied on, other than what follows from the above.
Results may differ from the reference program's by a relative error of at most 0.005.
Values may be sent and summed in bfloat16 or wider, within the bound.
A program may use at most 128 MiB of HBM per device.

```python
import math
import jax
import jax.numpy as jnp
from jax import lax

D = 2048
HEAD_COUNT = 16
HEAD_DIM = 128
TOK_DEV = 256
TOKEN_LENGTH = 1024


def head_slow(source, slow_count):
    head_order = jax.random.permutation(jax.random.fold_in(source, 101), HEAD_COUNT)
    return (head_order < slow_count).astype(jnp.float32)


def log_uniform(source, dims_shape, low_end, high_end):
    return jnp.exp(jax.random.uniform(source, dims_shape, jnp.float32, math.log(low_end), math.log(high_end)))


def draw_decay_rates(key, part):
    slow_count = HEAD_COUNT // 2
    slow_low = 0.1
    slow_high = 0.4
    slow_mask = head_slow(key, slow_count)
    slow_level = log_uniform(jax.random.fold_in(key, 1), (HEAD_COUNT,), slow_low, slow_high) / TOKEN_LENGTH
    fast_level = log_uniform(jax.random.fold_in(key, 2), (HEAD_COUNT,), 0.02, 0.05)
    baseline_intensity = slow_mask * slow_level + (1.0 - slow_mask) * fast_level
    token_multiplier = log_uniform(jax.random.fold_in(key, 3), (TOKEN_LENGTH, HEAD_COUNT), 0.5, 2.0)
    block_draw = log_uniform(jax.random.fold_in(key, 4), (TOKEN_LENGTH // TOK_DEV, HEAD_COUNT), 0.5, 2.0)
    block_multiplier = jnp.repeat(block_draw, TOK_DEV, axis=0)
    first_spike = jax.random.randint(jax.random.fold_in(key, 5), (HEAD_COUNT,), 0, TOKEN_LENGTH)
    spike_offset = jax.random.randint(jax.random.fold_in(key, 9), (HEAD_COUNT,), 1, TOKEN_LENGTH)
    second_spike = (first_spike + spike_offset) % TOKEN_LENGTH
    spike_position = jnp.stack([first_spike, second_spike], axis=0)
    spike_retention = jax.random.uniform(jax.random.fold_in(key, 6), (2, HEAD_COUNT), jnp.float32, 0.5, 0.8)
    token_positions = jnp.arange(TOKEN_LENGTH)[:, None, None]
    spike_intensity = jnp.sum(jnp.where(token_positions == spike_position[None], -jnp.log(spike_retention)[None], 0.0), axis=1)
    return (baseline_intensity[None, :] * token_multiplier * block_multiplier + spike_intensity).astype(jnp.float32)


def draw_reflect_betas(key, part):
    slow_count = HEAD_COUNT // 2
    fast_low = 0.3
    fast_high = 1.5
    slow_low = 0.4
    slow_high = 1.6
    slow_mask = head_slow(key, slow_count)
    slow_beta = 0.3 * HEAD_DIM / TOKEN_LENGTH * jax.random.uniform(jax.random.fold_in(key, 7), (TOKEN_LENGTH, 2, HEAD_COUNT), jnp.float32, slow_low, slow_high)
    fast_beta = jax.random.uniform(jax.random.fold_in(key, 8), (TOKEN_LENGTH, 2, HEAD_COUNT), jnp.float32, fast_low, fast_high)
    return jnp.where(slow_mask[None, None, :] > 0.5, slow_beta, fast_beta).astype(jnp.float32)


def touch_ends(entries, key, low, high):
    longest = entries.shape.index(max(entries.shape))
    spots = []
    for shift in (0, 1):
        where = [jax.random.randint(jax.random.fold_in(key, axis), (), 0, length) for axis, length in enumerate(entries.shape)]
        where[longest] = (where[longest] + shift) % entries.shape[longest]
        spots.append(tuple(where))
    return entries.at[spots[0]].set(low).at[spots[1]].set(high)


def steps_of(key, shape, cuts, smallest, high):
    level = 1.0
    for axis_at, blocks in cuts:
        heights = jax.random.uniform(jax.random.fold_in(jax.random.fold_in(key, 6), axis_at), (blocks,), jnp.float32, smallest / len(cuts), high / len(cuts))
        level = level * jnp.repeat(jnp.exp(heights), shape[axis_at] // blocks).reshape((-1,) + (1,) * (len(shape) - 1 - axis_at))
    return level


def bell_draw(key, dims, deviation, most, pieces=(), dtype=jnp.bfloat16):
    drawn = deviation * jax.random.normal(key, dims, jnp.float32)
    if pieces:
        drawn = drawn * steps_of(key, dims, pieces, -0.22, 0.18)
    return jnp.clip(drawn, -most, most).astype(dtype)


def setup_inputs(seed: int = 0, part: int = 0) -> dict:
    keys = jax.random.split(jax.random.key(seed), 9)
    part_splits = jax.random.split(jax.random.fold_in(keys[8], part), 9)
    queries = bell_draw(part_splits[0], (TOKEN_LENGTH, HEAD_COUNT * HEAD_DIM), 1.0, 6.0, ((0, 4), (1, 4)))
    reflect_keys = bell_draw(part_splits[1], (TOKEN_LENGTH, 2, HEAD_COUNT * HEAD_DIM), 1.0, 6.0, ((0, 4), (2, 4)))
    reflect_values = bell_draw(part_splits[2], (TOKEN_LENGTH, 2, HEAD_COUNT * HEAD_DIM), 1.0, 6.0, ((0, 4), (2, 4)))
    reflect_betas = draw_reflect_betas(jax.random.fold_in(jax.random.fold_in(keys[8], part), 71), part)
    decay_rates = draw_decay_rates(jax.random.fold_in(jax.random.fold_in(keys[8], part), 71), part)
    resets = touch_ends((jax.random.randint(part_splits[5], (TOKEN_LENGTH,), 0, TOKEN_LENGTH) < 2).astype(jnp.int32), jax.random.fold_in(part_splits[5], 1), 0, 1)
    out_weight = bell_draw(keys[6], (HEAD_COUNT * HEAD_DIM, D), (HEAD_COUNT * HEAD_DIM) ** -0.5, 0.125, ((0, 4),))
    out_cotangent = bell_draw(part_splits[7], (TOKEN_LENGTH, D), 1.0, 6.0, ((0, 4), (1, 4)))
    return {"queries": queries, "reflect_keys": reflect_keys, "reflect_values": reflect_values, "reflect_betas": reflect_betas, "decay_rates": decay_rates, "resets": resets, "out_weight": out_weight, "out_cotangent": out_cotangent}


MATMUL_ACCURACY = lax.Precision.HIGHEST

def normalize(raw):
    floats = raw.astype(jnp.float32)
    return floats * lax.rsqrt(lax.optimization_barrier(jnp.sum(floats * floats, axis=-1, keepdims=True)) + 1e-06)

def reflect(state_matrix, factor, beta, reflect_direction):
    projected_state = jnp.einsum('to,tof->tf', reflect_direction, state_matrix, precision=MATMUL_ACCURACY)
    return factor[:, None, None] * (state_matrix - beta[:, None, None] * reflect_direction[:, :, None] * projected_state[:, None, :])

def reference(queries, reflect_keys, reflect_values, reflect_betas, decay_rates, resets, out_weight, out_cotangent):
    queries_f = queries.astype(jnp.float32).reshape(TOKEN_LENGTH, HEAD_COUNT, HEAD_DIM)
    unit_keys = normalize(reflect_keys.reshape(TOKEN_LENGTH, 2, HEAD_COUNT, HEAD_DIM))
    values_f = reflect_values.astype(jnp.float32).reshape(TOKEN_LENGTH, 2, HEAD_COUNT, HEAD_DIM)
    gates = jnp.exp(-decay_rates)
    survive = jnp.broadcast_to((1 - resets).astype(jnp.float32)[:, None], (TOKEN_LENGTH, HEAD_COUNT))
    zeros_state = jnp.zeros((HEAD_COUNT, HEAD_DIM, HEAD_DIM), jnp.float32)

    def forward_token(state_matrix, inputs):
        query_vector, paired_keys, values_pair, paired_betas, gate, alive = inputs
        for member, factor in ((0, alive), (1, gate)):
            written = (paired_betas[member][:, None] * paired_keys[member])[:, :, None] * values_pair[member][:, None, :]
            state_matrix = reflect(state_matrix, factor, paired_betas[member], paired_keys[member]) + written
        return (state_matrix, jnp.einsum('to,tof->tf', query_vector, state_matrix, precision=MATMUL_ACCURACY))
    _, mixed_heads = lax.scan(forward_token, zeros_state, (queries_f, unit_keys, values_f, reflect_betas, gates, survive))
    heads_bf = mixed_heads.reshape(TOKEN_LENGTH, HEAD_COUNT * HEAD_DIM).astype(jnp.bfloat16)
    output_features = jnp.dot(heads_bf, out_weight, preferred_element_type=jnp.float32).astype(jnp.bfloat16).T
    upstream = jnp.dot(out_cotangent, out_weight.T, preferred_element_type=jnp.float32).reshape(TOKEN_LENGTH, HEAD_COUNT, HEAD_DIM)

    def backward_token(carried, inputs):
        query_vector, paired_keys, paired_betas, gate, alive, incoming = inputs
        second_reflection = carried + query_vector[:, :, None] * incoming[:, None, :]
        gradient_second = paired_betas[1][:, None] * jnp.einsum('to,tof->tf', paired_keys[1], second_reflection, precision=MATMUL_ACCURACY)
        first_reflection = reflect(second_reflection, gate, paired_betas[1], paired_keys[1])
        gradient_first = paired_betas[0][:, None] * jnp.einsum('to,tof->tf', paired_keys[0], first_reflection, precision=MATMUL_ACCURACY)
        carried = reflect(first_reflection, alive, paired_betas[0], paired_keys[0])
        return (carried, jnp.stack([gradient_first, gradient_second], axis=0))
    _, gradient = lax.scan(backward_token, zeros_state, (queries_f, unit_keys, reflect_betas, gates, survive, upstream), reverse=True)
    value_grads = gradient.reshape(TOKEN_LENGTH, 2, HEAD_COUNT * HEAD_DIM)
    return (output_features, value_grads)
```

```python
import functools
import jax
import jax.numpy as jnp
from jax import lax
from jax.experimental import pallas as pl
from jax.experimental.pallas import tpu as pltpu
from jax.sharding import PartitionSpec as P

HALF = 64
BLK = 2 * HALF
F32 = jnp.float32
BF16 = jnp.bfloat16
NN = (((1,), (0,)), ((), ()))
NT = (((1,), (1,)), ((), ()))
TN = (((0,), (0,)), ((), ()))
MESH = pl.DeviceIdType.MESH


def dot1(a, b, dims=NN):
    return lax.dot_general(a.astype(BF16), b.astype(BF16), dims, preferred_element_type=F32)


def halves(a):
    high = a.astype(BF16)
    return high, (a - high.astype(F32)).astype(BF16)


def dot3(a, b, dims=NN):
    ah, al = halves(a)
    bh, bl = halves(b)
    d = functools.partial(lax.dot_general, dimension_numbers=dims, preferred_element_type=F32)
    return d(ah, bh) + (d(ah, bl) + d(al, bh))


def thirds(a):
    top = a.astype(BF16)
    rest = a - top.astype(F32)
    middle = rest.astype(BF16)
    return jnp.concatenate([top, middle, (rest - middle.astype(F32)).astype(BF16)], axis=0)


def exact_dot(a, b):
    rows = a.shape[0]
    sums = dot1(thirds(a), b)
    return sums[:rows] + sums[rows:2 * rows] + sums[2 * rows:]


def iota(shape, axis):
    return lax.broadcasted_iota(jnp.int32, shape, axis)


def padded(parts, tokens):
    count = sum(p.shape[0] for p in parts)
    return jnp.concatenate(parts + [jnp.zeros((-count % 16, tokens), F32)], axis=0)


def schedules(decay, resets, betas):
    heads, tokens = decay.shape
    steps = 2 * tokens
    source, target = iota((tokens, 2 * tokens), 0), iota((tokens, 2 * tokens), 1)
    sums = exact_dot(padded([decay, resets], tokens), (source <= target) & (target < tokens)
                     | (source < target - tokens))
    inclusive, exclusive = sums[:, :tokens], sums[:, tokens:]
    even = padded([exclusive[:heads], inclusive[heads:heads + 1], betas[0]], tokens)
    odd = padded([inclusive[:heads + 1], betas[1]], tokens)
    source, target = iota((steps, steps), 0), iota((steps, steps), 1)
    spread = source == (target & 1) * tokens + (target >> 1)
    rows = exact_dot(jnp.concatenate([even, odd], axis=1), spread)
    return rows, rows.T, inclusive.T


def local(hs, heads, schedule, q_ref, k_refs, v_refs, y_ref, r_ref, m_ref, o_ref, b_ref, between):
    rows, cols, tok_cols = schedule
    tokens = q_ref.shape[0]
    width = m_ref.shape[1]
    blocks = tokens // HALF
    steps = 2 * tokens
    everything = [(h, b) for h in hs for b in range(blocks)]
    z_row, z_col, z_tok = rows[heads:heads + 1], cols[:, heads:heads + 1], tok_cols[:, heads:heads + 1]
    c_row = {h: rows[h:h + 1] for h in hs}
    c_col = {h: cols[:, h:h + 1] for h in hs}
    c_tok = {h: tok_cols[:, h:h + 1] for h in hs}
    beta_row = {h: rows[heads + 1 + h:heads + 2 + h] for h in hs}
    beta_col = {h: cols[:, heads + 1 + h:heads + 2 + h] for h in hs}
    z_end = z_row[:, steps - 1:]

    def sl(b):
        return slice(b * BLK, (b + 1) * BLK)

    def ts(b):
        return slice(b * HALF, (b + 1) * HALF)

    def lanes(h):
        return slice(h * width, (h + 1) * width)

    keys = {(h, b): k_refs[h][sl(b), :] for h, b in everything}
    tm_r, tm_c = iota((BLK, BLK), 0), iota((BLK, BLK), 1)
    eye = tm_r == tm_c
    identity = jnp.where(eye, 1.0, 0.0)

    low, scale_row, scale_col, gram = {}, {}, {}, {}
    for h, b in everything:
        for c in range(b + 1):
            gram[h, b, c] = dot1(keys[h, b], keys[h, c], NT)
    for h, b in everything:
        diag = jnp.where(eye, gram[h, b, b], 0.0)
        scale_row[h, b] = lax.rsqrt(jnp.sum(diag, axis=0, keepdims=True) + 1e-6)
        scale_col[h, b] = lax.rsqrt(jnp.sum(diag, axis=1, keepdims=True) + 1e-6)
    for h, b in everything:
        left = beta_col[h][sl(b)] * scale_col[h, b]
        for c in range(b + 1):
            valid = z_col[sl(b)] == z_row[:, sl(c)]
            if b == c:
                valid = valid & (tm_r > tm_c)
            gap = jnp.where(valid, c_row[h][:, sl(c)] - c_col[h][sl(b)], 0.0)
            low[h, b, c] = jnp.where(
                valid, jnp.exp(gap) * gram[h, b, c] * left * scale_row[h, c], 0.0)

    rounded = {i: low[i[0], i[1], i[1]].astype(BF16) for i in everything}
    inverse = {i: identity - jnp.where((tm_r >> 1) == (tm_c >> 1), low[i[0], i[1], i[1]], 0.0)
               for i in everything}
    level = 2
    while (1 << level) <= BLK:
        pick = ((tm_r >> level) == (tm_c >> level)) & ((tm_r >> (level - 1)) != (tm_c >> (level - 1)))
        narrow = {i: inverse[i].astype(BF16) for i in everything}
        inner = {i: dot1(jnp.where(pick, rounded[i], jnp.zeros_like(rounded[i])), narrow[i])
                 for i in everything}
        inverse = {i: inverse[i] - dot1(narrow[i], inner[i]) for i in everything}
        level += 1
    for _ in range(2):
        residual = {i: dot3(low[i[0], i[1], i[1]], inverse[i]) + (inverse[i] - identity)
                    for i in everything}
        inverse = {i: inverse[i] - dot1(inverse[i], residual[i]) for i in everything}
    between()

    gamma_end_row = {h: jnp.where(z_row == z_end, jnp.exp(c_row[h] - c_row[h][:, steps - 1:]), 0.0)
                     for h in hs}
    solved = {}
    for b in reversed(range(blocks)):
        for h in hs:
            parts = []
            for a in range(b, blocks):
                product = dot1(q_ref[ts(a), lanes(h)], keys[h, b], NT)
                valid = z_tok[ts(a)] == z_row[:, sl(b)]
                if a == b:
                    valid = valid & (iota((HALF, BLK), 0) >= (iota((HALF, BLK), 1) >> 1))
                gap = jnp.where(valid, c_row[h][:, sl(b)] - c_tok[h][ts(a)], 0.0)
                parts.append(jnp.where(valid, jnp.exp(gap) * product * scale_row[h, b], 0.0))
            parts.append(keys[h, b].astype(F32).T * (scale_row[h, b] * gamma_end_row[h][:, sl(b)]))
            x = jnp.concatenate(parts, axis=0)
            if b + 1 < blocks:
                later = []
                for c in range(b + 1, blocks):
                    later.append(jnp.concatenate(
                        [jnp.zeros(((c - b) * HALF, BLK), F32), solved[h, c]], axis=0))
                x = x - dot3(jnp.concatenate(later, axis=1),
                             jnp.concatenate([low[h, c, b] for c in range(b + 1, blocks)], axis=0))
            solved[h, b] = dot3(x, inverse[h, b])

    for h in hs:
        gamma_row = jnp.where(z_row == 0, jnp.exp(-c_row[h]), 0.0)
        plain, moved = [], []
        for b in range(blocks):
            y = solved[h, b] * beta_row[h][:, sl(b)]
            if b:
                y = jnp.concatenate([jnp.zeros((b * HALF, BLK), F32), y], axis=0)
            plain.append(y.astype(BF16))
            moved.append((y * (gamma_row[:, sl(b)] * scale_row[h, b])).astype(BF16))
            y_ref[h, :, sl(b)] = plain[b]
        plain = dot1(jnp.concatenate(plain, axis=1), v_refs[h][...])
        moved = dot1(jnp.concatenate(moved, axis=1), k_refs[h][...])
        o_ref[h] = plain[:tokens]
        b_ref[h] = plain[tokens:]
        gamma_tok = jnp.where(z_tok == 0, jnp.exp(-c_tok[h]), 0.0)
        r_ref[h] = (gamma_tok * q_ref[:, lanes(h)].astype(F32) - moved[:tokens]).astype(BF16)
        gamma_end = jnp.where(z_end == 0, jnp.exp(-c_row[h][:, steps - 1:]), 0.0)
        m_ref[h] = jnp.where(iota((width, width), 0) == iota((width, width), 1), gamma_end, 0.0) - moved[tokens:]


def layer_kernel(devices, sections, decay_ref, beta_ref, reset_ref, q_hbm, k_hbm, v_hbm, w_hbm, cot_hbm,
                 out_hbm, g_hbm,
                 q_ref, k_ref, v_ref, w_ref, cot_ref, m_ref, b_ref, r_ref, o_ref, y_ref, g_ref, out_ref,
                 s_in, s_out, ds_in, ds_out, d, up_,
                 mixed, pair_out, pair_in, cross_out, cross_in,
                 k_loaded, v_loaded, loaded, stored,
                 s_sent, s_got, ds_sent, ds_got, pair_sent, pair_got, cross_sent, cross_got,
                 near_sent, near_got, far_sent, far_got):
    heads, tokens, width = r_ref.shape
    features = out_ref.shape[0]
    share = cot_hbm.shape[1]
    place = lax.axis_index("seq")
    section, core = lax.axis_index("section"), lax.axis_index("head")
    sibling = 1 - core
    first, last = place == 0, place == devices - 1

    def peer(k):
        return lax.rem(section + k, sections)

    def owned(part, side):
        return pl.ds(pl.multiple_of((part * 2 + side) * share, 128), share)

    barrier = pltpu.get_barrier_semaphore()

    @pl.when(jnp.logical_not(first))
    def _():
        pl.semaphore_signal(barrier, inc=1, device_id={"seq": place - 1}, device_id_type=MESH)

    @pl.when(jnp.logical_not(last))
    def _():
        pl.semaphore_signal(barrier, inc=1, device_id={"seq": place + 1}, device_id_type=MESH)

    pl.semaphore_signal(barrier, inc=1, device_id={"head": sibling}, device_id_type=MESH)
    for k in range(1, sections):
        pl.semaphore_signal(barrier, inc=1, device_id={"section": peer(k)}, device_id_type=MESH)

    def strip(h):
        return pl.ds(h * width, width)

    k_loads = [pltpu.make_async_copy(k_hbm.at[:, :, strip(h)], k_ref.at[h], k_loaded.at[h]) for h in range(heads)]
    v_loads = [pltpu.make_async_copy(v_hbm.at[:, :, strip(h)], v_ref.at[h], v_loaded.at[h]) for h in range(heads)]
    q_load = pltpu.make_async_copy(q_hbm, q_ref, loaded.at[0])
    w_load = pltpu.make_async_copy(w_hbm, w_ref, loaded.at[1])
    cot_load = pltpu.make_async_copy(cot_hbm, cot_ref.at[:, owned(section, core)], loaded.at[2])
    for load in k_loads + [q_load] + v_loads + [cot_load, w_load]:
        load.start()

    def far(k):
        return pltpu.make_async_remote_copy(
            src_ref=cot_hbm, dst_ref=cot_ref.at[:, owned(section, core)],
            send_sem=far_sent.at[k - 1], recv_sem=far_got.at[k - 1],
            device_id={"section": peer(k)}, device_id_type=MESH)

    def near(k):
        block = owned(peer(sections - k), core)
        return pltpu.make_async_remote_copy(
            src_ref=cot_ref.at[:, block] if k else cot_hbm, dst_ref=cot_ref.at[:, block],
            send_sem=near_sent.at[k], recv_sem=near_got.at[k],
            device_id={"head": sibling}, device_id_type=MESH)

    pl.semaphore_wait(barrier, sections + jnp.where(first, 0, 1) + jnp.where(last, 0, 1))
    for k in range(1, sections):
        far(k).start()
    near(0).start()

    schedule = schedules(decay_ref[...], reset_ref[...].astype(F32), beta_ref[...])
    k_refs = [k_ref.at[h].reshape(2 * tokens, width) for h in range(heads)]
    v_refs = [v_ref.at[h].reshape(2 * tokens, width) for h in range(heads)]
    q_load.wait()

    def up(h):
        return pltpu.make_async_remote_copy(
            src_ref=s_out.at[h], dst_ref=s_in.at[h], send_sem=s_sent.at[h], recv_sem=s_got.at[h],
            device_id={"seq": place + 1}, device_id_type=MESH)

    def down(h):
        return pltpu.make_async_remote_copy(
            src_ref=ds_out.at[h], dst_ref=ds_in.at[h], send_sem=ds_sent.at[h], recv_sem=ds_got.at[h],
            device_id={"seq": place - 1}, device_id_type=MESH)

    def forward():
        for h in range(heads):
            @pl.when(first)
            def _():
                s_in[h] = jnp.zeros(s_in.shape[1:], BF16)

            @pl.when(jnp.logical_not(first))
            def _():
                up(h).wait_recv()

            @pl.when(jnp.logical_not(last))
            def _():
                s = s_in[h]
                mh, ml = halves(m_ref[h])
                s_out[h] = (dot1(mh, s) + dot1(ml, s) + b_ref[h]).astype(BF16)
                up(h).start()

    def backward():
        for h in range(heads):
            @pl.when(last)
            def _():
                ds_in[h] = jnp.zeros(ds_in.shape[1:], BF16)

            @pl.when(jnp.logical_not(last))
            def _():
                down(h).wait_recv()

            @pl.when(jnp.logical_not(first))
            def _():
                ds = ds_in[h]
                mh, ml = halves(m_ref[h])
                ds_out[h] = (dot1(mh, ds, TN) + dot1(ml, ds, TN) + d[h]).astype(BF16)
                down(h).start()

    def relay():
        for k in range(1, sections):
            far(k).wait_recv()
            near(k).start()

    def upstreams():
        w_load.wait()
        cot_load.wait()
        for k in range(sections):
            near(k).wait_recv()
        for h in range(heads):
            up_[h] = dot1(cot_ref[...], w_ref[h * width:(h + 1) * width, :], NT).astype(BF16)

    group = GROUP if heads % GROUP == 0 else heads
    groups = [list(range(h, h + group)) for h in range(0, heads, group)]
    for i, hs in enumerate(groups):
        for h in hs:
            k_loads[h].wait()
            v_loads[h].wait()

        def between(i=i):
            if i == 0:
                relay()
            if i == len(groups) - 1:
                upstreams()

        local(hs, heads, schedule, q_ref, k_refs, v_refs, y_ref, r_ref, m_ref, o_ref, b_ref, between)

    low = 2 * place < devices

    @pl.when(low)
    def _():
        forward()

    for h in range(heads):
        d[h] = dot1(r_ref[h], up_[h], TN)

    @pl.when(low)
    def _():
        backward()

    @pl.when(jnp.logical_not(low))
    def _():
        backward()
        forward()

    for h in range(heads):
        mixed[h * width:(h + 1) * width, :] = (dot1(r_ref[h], s_in[h]) + o_ref[h]).T.astype(BF16)

    def partial(target, side):
        start = pl.multiple_of((target * 2 + side) * features, 128)
        return dot1(w_ref[:, pl.ds(start, features)], mixed[...], TN)

    def pair(k):
        return pltpu.make_async_remote_copy(
            src_ref=pair_out.at[k], dst_ref=pair_in.at[k], send_sem=pair_sent.at[k],
            recv_sem=pair_got.at[k], device_id={"head": sibling}, device_id_type=MESH)

    def cross(k):
        return pltpu.make_async_remote_copy(
            src_ref=cross_out.at[k - 1], dst_ref=cross_in.at[k - 1], send_sem=cross_sent.at[k - 1],
            recv_sem=cross_got.at[k - 1], device_id={"section": peer(k)}, device_id_type=MESH)

    for k in range(1, sections):
        pair_out[k] = partial(peer(k), sibling)
        pair(k).start()
    for k in range(1, sections):
        mine = partial(peer(k), core)
        pair(k).wait_recv()
        cross_out[k - 1] = (mine + pair_in[k]).astype(BF16)
        cross(k).start()
    pair_out[0] = partial(section, sibling)
    pair(0).start()

    def g_store(h):
        return pltpu.make_async_copy(g_ref.at[h], g_hbm.at[:, :, strip(h)], stored.at[h])

    for h in range(heads):
        right = jnp.concatenate([up_[h], ds_in[h]], axis=0)
        g_ref.at[h].reshape(2 * tokens, width)[...] = dot1(y_ref[h], right, TN)
        g_store(h).start()
    total = partial(section, core)
    pair(0).wait_recv()
    total = total + pair_in[0]
    for k in range(1, sections):
        cross(k).wait_recv()
        total = total + cross_in[k - 1].astype(F32)
    out_ref[...] = total.astype(BF16)
    out_store = pltpu.make_async_copy(out_ref, out_hbm, stored.at[heads])
    out_store.start()
    for k in range(sections):
        pair(k).wait_send()
        near(k).wait_send()
    for k in range(1, sections):
        cross(k).wait_send()
        far(k).wait_send()

    @pl.when(jnp.logical_not(last))
    def _():
        for h in range(heads):
            up(h).wait_send()

    @pl.when(jnp.logical_not(first))
    def _():
        for h in range(heads):
            down(h).wait_send()

    for h in range(heads):
        g_store(h).wait()
    out_store.wait()


GROUP = 2
PIECES = 4


def results_kernel(out_in, g_in, out_ref, g_ref, done):
    rows = g_in.shape[0] // PIECES
    copies = [pltpu.make_async_copy(out_in, out_ref, done.at[PIECES])]
    for i in range(PIECES):
        part = pl.ds(i * rows, rows)
        copies.append(pltpu.make_async_copy(g_in.at[part], g_ref.at[part], done.at[i]))
    for copy in copies:
        copy.start()
    for copy in copies:
        copy.wait()


def per_device(queries, reflect_keys, reflect_values, reflect_betas, decay_rates, resets,
               out_weight, out_cotangent):
    tokens = queries.shape[0]
    heads = reflect_betas.shape[2]
    width = queries.shape[1] // heads
    steps = 2 * tokens
    devices = lax.axis_size("seq")
    sections = lax.axis_size("section")
    features = out_weight.shape[1] // (2 * sections)
    total = tokens + width

    square = (heads, width, width)
    pairs = (heads, tokens, 2, width)
    vmem = pl.BlockSpec(memory_space=pltpu.VMEM)
    hbm = pl.BlockSpec(memory_space=pl.ANY)
    dma = pltpu.SemaphoreType.DMA
    shapes = [jax.ShapeDtypeStruct((features, tokens), BF16),
              jax.ShapeDtypeStruct((tokens, 2, heads * width), F32)]
    output, value_grads = pl.pallas_call(
        functools.partial(layer_kernel, devices, sections),
        in_specs=[vmem] * 3 + [hbm] * 5,
        out_specs=[hbm] * 2,
        out_shape=shapes,
        scratch_shapes=[pltpu.VMEM(queries.shape, BF16), pltpu.VMEM(pairs, BF16), pltpu.VMEM(pairs, BF16),
                        pltpu.VMEM(out_weight.shape, BF16), pltpu.VMEM((tokens, out_weight.shape[1]), BF16),
                        pltpu.VMEM(square, F32), pltpu.VMEM(square, F32),
                        pltpu.VMEM((heads, tokens, width), BF16), pltpu.VMEM((heads, tokens, width), F32),
                        pltpu.VMEM((heads, total, steps), BF16), pltpu.VMEM(pairs, F32),
                        pltpu.VMEM((features, tokens), BF16)]
        + [pltpu.VMEM(square, BF16)] * 4
        + [pltpu.VMEM(square, F32), pltpu.VMEM((heads, tokens, width), BF16)]
        + [pltpu.VMEM((heads * width, tokens), BF16),
           pltpu.VMEM((sections, features, tokens), F32),
           pltpu.VMEM((sections, features, tokens), F32),
           pltpu.VMEM((sections - 1, features, tokens), BF16),
           pltpu.VMEM((sections - 1, features, tokens), BF16)]
        + [dma((heads,)), dma((heads,)), dma((3,)), dma((heads + 1,))]
        + [dma((heads,))] * 4 + [dma((sections,))] * 2 + [dma((sections - 1,))] * 2
        + [dma((sections,))] * 2 + [dma((sections - 1,))] * 2,
        compiler_params=pltpu.CompilerParams(
            collective_id=0, has_side_effects=True, vmem_limit_bytes=58 << 20),
        name="layer",
    )(decay_rates.T, reflect_betas.transpose(1, 2, 0), resets.reshape(1, tokens),
      queries, reflect_keys, reflect_values, out_weight, out_cotangent)
    return pl.pallas_call(
        results_kernel,
        in_specs=[hbm] * 2,
        out_specs=[hbm] * 2,
        out_shape=shapes,
        scratch_shapes=[dma((PIECES + 1,))],
        name="results",
    )(output, value_grads)


def solution(mesh):
    return jax.shard_map(
        per_device,
        mesh=mesh,
        in_specs=(
            P(("grp", "seq"), ("section", "head")),
            P(("grp", "seq"), None, ("section", "head")),
            P(("grp", "seq"), None, ("section", "head")),
            P(("grp", "seq"), None, ("section", "head")),
            P(("grp", "seq"), ("section", "head")),
            P(("grp", "seq")),
            P(("section", "head"), None),
            P(("grp", "seq"), ("section", "head")),
        ),
        out_specs=(
            P(("section", "head"), ("grp", "seq")),
            P(("grp", "seq"), None, ("section", "head")),
        ),
        check_vma=False,
    )
```

```python
import functools
import jax
import jax.numpy as jnp
from jax import lax
from jax.experimental import pallas as pl
from jax.experimental.pallas import tpu as pltpu
from jax.sharding import PartitionSpec as P

HALF = 64
BLK = 2 * HALF
F32 = jnp.float32
BF16 = jnp.bfloat16
NN = (((1,), (0,)), ((), ()))
NT = (((1,), (1,)), ((), ()))
TN = (((0,), (0,)), ((), ()))
MESH = pl.DeviceIdType.MESH


def dot1(a, b, dims=NN):
    return lax.dot_general(a.astype(BF16), b.astype(BF16), dims, preferred_element_type=F32)


def halves(a):
    high = a.astype(BF16)
    return high, (a - high.astype(F32)).astype(BF16)


def dot3(a, b, dims=NN):
    ah, al = halves(a)
    bh, bl = halves(b)
    d = functools.partial(lax.dot_general, dimension_numbers=dims, preferred_element_type=F32)
    return d(ah, bh) + (d(ah, bl) + d(al, bh))


def thirds(a):
    top = a.astype(BF16)
    rest = a - top.astype(F32)
    middle = rest.astype(BF16)
    return jnp.concatenate([top, middle, (rest - middle.astype(F32)).astype(BF16)], axis=0)


def exact_dot(a, b):
    rows = a.shape[0]
    sums = dot1(thirds(a), b)
    return sums[:rows] + sums[rows:2 * rows] + sums[2 * rows:]


def iota(shape, axis):
    return lax.broadcasted_iota(jnp.int32, shape, axis)


def padded(parts, tokens):
    count = sum(p.shape[0] for p in parts)
    return jnp.concatenate(parts + [jnp.zeros((-count % 16, tokens), F32)], axis=0)


def schedules(decay, resets, betas):
    heads, tokens = decay.shape
    steps = 2 * tokens
    source, target = iota((tokens, 2 * tokens), 0), iota((tokens, 2 * tokens), 1)
    sums = exact_dot(padded([decay, resets], tokens), (source <= target) & (target < tokens)
                     | (source < target - tokens))
    inclusive, exclusive = sums[:, :tokens], sums[:, tokens:]
    even = padded([exclusive[:heads], inclusive[heads:heads + 1], betas[0]], tokens)
    odd = padded([inclusive[:heads + 1], betas[1]], tokens)
    source, target = iota((steps, steps), 0), iota((steps, steps), 1)
    spread = source == (target & 1) * tokens + (target >> 1)
    rows = exact_dot(jnp.concatenate([even, odd], axis=1), spread)
    return rows, rows.T, inclusive.T


def local(heads, schedule, q_ref, k_refs, v_refs, yq_ref, yk_ref, r_ref, m_ref, o_ref, b_ref, between):
    rows, cols, tok_cols = schedule
    tokens = q_ref.shape[0]
    width = m_ref.shape[1]
    blocks = tokens // HALF
    steps = 2 * tokens
    everything = [(h, b) for h in range(heads) for b in range(blocks)]
    z_row, z_col, z_tok = rows[heads:heads + 1], cols[:, heads:heads + 1], tok_cols[:, heads:heads + 1]
    c_row = [rows[h:h + 1] for h in range(heads)]
    c_col = [cols[:, h:h + 1] for h in range(heads)]
    c_tok = [tok_cols[:, h:h + 1] for h in range(heads)]
    beta_row = [rows[heads + 1 + h:heads + 2 + h] for h in range(heads)]
    beta_col = [cols[:, heads + 1 + h:heads + 2 + h] for h in range(heads)]
    z_end = z_row[:, steps - 1:]

    def sl(b):
        return slice(b * BLK, (b + 1) * BLK)

    def ts(b):
        return slice(b * HALF, (b + 1) * HALF)

    def lanes(h):
        return slice(h * width, (h + 1) * width)

    keys = {(h, b): k_refs[h][sl(b), :] for h, b in everything}
    tm_r, tm_c = iota((BLK, BLK), 0), iota((BLK, BLK), 1)
    eye = tm_r == tm_c
    identity = jnp.where(eye, 1.0, 0.0)

    low, scale_row, scale_col, gram = {}, {}, {}, {}
    for h, b in everything:
        for c in range(b + 1):
            gram[h, b, c] = dot1(keys[h, b], keys[h, c], NT)
    for h, b in everything:
        diag = jnp.where(eye, gram[h, b, b], 0.0)
        scale_row[h, b] = lax.rsqrt(jnp.sum(diag, axis=0, keepdims=True) + 1e-6)
        scale_col[h, b] = lax.rsqrt(jnp.sum(diag, axis=1, keepdims=True) + 1e-6)
    for h, b in everything:
        left = beta_col[h][sl(b)] * scale_col[h, b]
        for c in range(b + 1):
            valid = z_col[sl(b)] == z_row[:, sl(c)]
            if b == c:
                valid = valid & (tm_r > tm_c)
            gap = jnp.where(valid, c_row[h][:, sl(c)] - c_col[h][sl(b)], 0.0)
            low[h, b, c] = jnp.where(
                valid, jnp.exp(gap) * gram[h, b, c] * left * scale_row[h, c], 0.0)

    rounded = {i: low[i[0], i[1], i[1]].astype(BF16) for i in everything}
    inverse = {i: identity - jnp.where((tm_r >> 1) == (tm_c >> 1), low[i[0], i[1], i[1]], 0.0)
               for i in everything}
    level = 2
    while (1 << level) <= BLK:
        pick = ((tm_r >> level) == (tm_c >> level)) & ((tm_r >> (level - 1)) != (tm_c >> (level - 1)))
        narrow = {i: inverse[i].astype(BF16) for i in everything}
        inner = {i: dot1(jnp.where(pick, rounded[i], jnp.zeros_like(rounded[i])), narrow[i])
                 for i in everything}
        inverse = {i: inverse[i] - dot1(narrow[i], inner[i]) for i in everything}
        level += 1
    for _ in range(2):
        residual = {i: dot3(low[i[0], i[1], i[1]], inverse[i]) + (inverse[i] - identity)
                    for i in everything}
        inverse = {i: inverse[i] - dot1(inverse[i], residual[i]) for i in everything}
    between()

    gamma_row = [jnp.where(z_row == 0, jnp.exp(-c_row[h]), 0.0) for h in range(heads)]

    def solve(hs, right):
        solved = {}
        for b in reversed(range(blocks)):
            for h in hs:
                x = right(h, b)
                if b + 1 < blocks:
                    later = []
                    for c in range(b + 1, blocks):
                        short = x.shape[0] - solved[h, c].shape[0]
                        later.append(jnp.concatenate([jnp.zeros((short, BLK), F32), solved[h, c]], axis=0)
                                     if short else solved[h, c])
                    x = x - dot3(jnp.concatenate(later, axis=1),
                                 jnp.concatenate([low[h, c, b] for c in range(b + 1, blocks)], axis=0))
                solved[h, b] = dot3(x, inverse[h, b])
        return solved

    def products(h, solved, y_ref):
        plain, moved = [], []
        for b in range(blocks):
            y = solved[h, b] * beta_row[h][:, sl(b)]
            short = y_ref.shape[1] - y.shape[0]
            if short:
                y = jnp.concatenate([jnp.zeros((short, BLK), F32), y], axis=0)
            plain.append(y.astype(BF16))
            moved.append((y * (gamma_row[h][:, sl(b)] * scale_row[h, b])).astype(BF16))
            y_ref[h, :, sl(b)] = plain[b]
        return (dot1(jnp.concatenate(plain, axis=1), v_refs[h][...]),
                dot1(jnp.concatenate(moved, axis=1), k_refs[h][...]))

    gamma_end_row = [jnp.where(z_row == z_end, jnp.exp(c_row[h] - c_row[h][:, steps - 1:]), 0.0)
                     for h in range(heads)]

    def end_side(h, b):
        return keys[h, b].astype(F32).T * (scale_row[h, b] * gamma_end_row[h][:, sl(b)])

    def token_side(h, b):
        parts = []
        for a in range(b, blocks):
            product = dot1(q_ref[ts(a), lanes(h)], keys[h, b], NT)
            valid = z_tok[ts(a)] == z_row[:, sl(b)]
            if a == b:
                valid = valid & (iota((HALF, BLK), 0) >= (iota((HALF, BLK), 1) >> 1))
            gap = jnp.where(valid, c_row[h][:, sl(b)] - c_tok[h][ts(a)], 0.0)
            parts.append(jnp.where(valid, jnp.exp(gap) * product * scale_row[h, b], 0.0))
        return jnp.concatenate(parts, axis=0)

    solved = solve(range(heads), end_side)
    for h in range(heads):
        plain, moved = products(h, solved, yk_ref)
        gamma_end = jnp.where(z_end == 0, jnp.exp(-c_row[h][:, steps - 1:]), 0.0)
        b_ref[h] = plain
        m_ref[h] = jnp.where(iota((width, width), 0) == iota((width, width), 1), gamma_end, 0.0) - moved

    def tokens_of(hs):
        solved = solve(hs, token_side)
        for h in hs:
            plain, moved = products(h, solved, yq_ref)
            o_ref[h] = plain
            gamma_tok = jnp.where(z_tok == 0, jnp.exp(-c_tok[h]), 0.0)
            r_ref[h] = (gamma_tok * q_ref[:, lanes(h)].astype(F32) - moved).astype(BF16)

    return tokens_of


def layer_kernel(devices, sections, decay_ref, beta_ref, reset_ref, q_hbm, k_hbm, v_hbm, w_hbm, cot_hbm,
                 out_hbm, g_hbm,
                 q_ref, k_ref, v_ref, w_ref, cot_ref, m_ref, b_ref, r_ref, o_ref, yq_ref, yk_ref, g_ref, out_ref,
                 s_in, s_out, ds_in, ds_out, d, up_,
                 mixed, own, pair_out, pair_in, cross_out, cross_in,
                 k_loaded, v_loaded, loaded, stored,
                 s_sent, s_got, ds_sent, ds_got, pair_sent, pair_got, cross_sent, cross_got,
                 near_sent, near_got, far_sent, far_got):
    heads, tokens, width = r_ref.shape
    features = out_ref.shape[0]
    share = cot_hbm.shape[1]
    place = lax.axis_index("seq")
    section, core = lax.axis_index("section"), lax.axis_index("head")
    sibling = 1 - core
    first, last = place == 0, place == devices - 1

    def peer(k):
        return lax.rem(section + k, sections)

    def owned(part, side):
        return pl.ds(pl.multiple_of((part * 2 + side) * share, 128), share)

    barrier = pltpu.get_barrier_semaphore()

    @pl.when(jnp.logical_not(first))
    def _():
        pl.semaphore_signal(barrier, inc=1, device_id={"seq": place - 1}, device_id_type=MESH)

    @pl.when(jnp.logical_not(last))
    def _():
        pl.semaphore_signal(barrier, inc=1, device_id={"seq": place + 1}, device_id_type=MESH)

    pl.semaphore_signal(barrier, inc=1, device_id={"head": sibling}, device_id_type=MESH)
    for k in range(1, sections):
        pl.semaphore_signal(barrier, inc=1, device_id={"section": peer(k)}, device_id_type=MESH)

    def strip(h):
        return pl.ds(h * width, width)

    k_loads = [pltpu.make_async_copy(k_hbm.at[:, :, strip(h)], k_ref.at[h], k_loaded.at[h]) for h in range(heads)]
    v_loads = [pltpu.make_async_copy(v_hbm.at[:, :, strip(h)], v_ref.at[h], v_loaded.at[h]) for h in range(heads)]
    q_load = pltpu.make_async_copy(q_hbm, q_ref, loaded.at[0])
    w_load = pltpu.make_async_copy(w_hbm, w_ref, loaded.at[1])
    cot_load = pltpu.make_async_copy(cot_hbm, cot_ref.at[:, owned(section, core)], loaded.at[2])
    for load in k_loads + v_loads + [q_load, cot_load, w_load]:
        load.start()

    def far(k):
        return pltpu.make_async_remote_copy(
            src_ref=cot_hbm, dst_ref=cot_ref.at[:, owned(section, core)],
            send_sem=far_sent.at[k - 1], recv_sem=far_got.at[k - 1],
            device_id={"section": peer(k)}, device_id_type=MESH)

    def near(k):
        block = owned(peer(sections - k), core)
        return pltpu.make_async_remote_copy(
            src_ref=cot_ref.at[:, block] if k else cot_hbm, dst_ref=cot_ref.at[:, block],
            send_sem=near_sent.at[k], recv_sem=near_got.at[k],
            device_id={"head": sibling}, device_id_type=MESH)

    pl.semaphore_wait(barrier, sections + jnp.where(first, 0, 1) + jnp.where(last, 0, 1))
    for k in range(1, sections):
        far(k).start()
    near(0).start()

    schedule = schedules(decay_ref[...], reset_ref[...].astype(F32), beta_ref[...])
    k_refs = [k_ref.at[h].reshape(2 * tokens, width) for h in range(heads)]
    v_refs = [v_ref.at[h].reshape(2 * tokens, width) for h in range(heads)]

    def up(h):
        return pltpu.make_async_remote_copy(
            src_ref=s_out.at[h], dst_ref=s_in.at[h], send_sem=s_sent.at[h], recv_sem=s_got.at[h],
            device_id={"seq": place + 1}, device_id_type=MESH)

    def down(h):
        return pltpu.make_async_remote_copy(
            src_ref=ds_out.at[h], dst_ref=ds_in.at[h], send_sem=ds_sent.at[h], recv_sem=ds_got.at[h],
            device_id={"seq": place - 1}, device_id_type=MESH)

    def forward():
        for h in range(heads):
            up(h).wait_recv()

            @pl.when(jnp.logical_not(last))
            def _():
                s = s_in[h]
                mh, ml = halves(m_ref[h])
                s_out[h] = (dot1(mh, s) + dot1(ml, s) + b_ref[h]).astype(BF16)
                up(h).start()

    def backward():
        for h in range(heads):
            @pl.when(last)
            def _():
                ds_in[h] = jnp.zeros(ds_in.shape[1:], BF16)

            @pl.when(jnp.logical_not(last))
            def _():
                down(h).wait_recv()

            @pl.when(jnp.logical_not(first))
            def _():
                ds = ds_in[h]
                mh, ml = halves(m_ref[h])
                ds_out[h] = (dot1(mh, ds, TN) + dot1(ml, ds, TN) + d[h]).astype(BF16)
                down(h).start()

    def relay():
        for k in range(1, sections):
            far(k).wait_recv()
            near(k).start()

    for load in k_loads + v_loads + [q_load]:
        load.wait()
    tokens_of = local(heads, schedule, q_ref, k_refs, v_refs, yq_ref, yk_ref, r_ref, m_ref, o_ref, b_ref, relay)

    @pl.when(first)
    def _():
        for h in range(heads):
            s_in[h] = jnp.zeros(s_in.shape[1:], BF16)
            s_out[h] = b_ref[h].astype(BF16)
            up(h).start()

    tokens_of(range(heads // 2))
    w_load.wait()
    cot_load.wait()
    for k in range(sections):
        near(k).wait_recv()
    up_[...] = dot1(cot_ref[...], w_ref[...], NT).astype(BF16)

    @pl.when(place == 1)
    def _():
        forward()

    tokens_of(range(heads // 2, heads))
    for h in range(heads):
        d[h] = dot1(r_ref[h], up_[:, strip(h)], TN)
    high = 2 * place > devices

    @pl.when(high)
    def _():
        backward()

    @pl.when(place > 1)
    def _():
        forward()

    for h in range(heads):
        mixed[:, strip(h)] = (dot1(r_ref[h], s_in[h]) + o_ref[h]).astype(BF16)

    def partial(target, side):
        start = pl.multiple_of((target * 2 + side) * features, 128)
        return dot1(mixed[...], w_ref[:, pl.ds(start, features)])

    def pair(k):
        return pltpu.make_async_remote_copy(
            src_ref=pair_out.at[k], dst_ref=pair_in.at[k], send_sem=pair_sent.at[k],
            recv_sem=pair_got.at[k], device_id={"head": sibling}, device_id_type=MESH)

    def cross(k):
        return pltpu.make_async_remote_copy(
            src_ref=cross_out.at[k - 1], dst_ref=cross_in.at[k - 1], send_sem=cross_sent.at[k - 1],
            recv_sem=cross_got.at[k - 1], device_id={"section": peer(k)}, device_id_type=MESH)

    for k in range(1, sections):
        pair_out[k] = partial(peer(k), sibling)
        pair(k).start()
    for k in range(1, sections):
        mine = partial(peer(k), core)
        pair(k).wait_recv()
        cross_out[k - 1] = (mine + pair_in[k]).astype(BF16)
        cross(k).start()
    pair_out[0] = partial(section, sibling)
    pair(0).start()

    def g_store(h):
        return pltpu.make_async_copy(g_ref.at[h], g_hbm.at[:, :, strip(h)], stored.at[h])

    g_refs = [g_ref.at[h].reshape(2 * tokens, width) for h in range(heads)]
    for h in range(heads):
        g_refs[h][...] = dot1(yq_ref[h], up_[:, strip(h)], TN)
    total = partial(section, core)
    pair(0).wait_recv()
    own[...] = total + pair_in[0]

    @pl.when(jnp.logical_not(high))
    def _():
        backward()

    for h in range(heads):
        g_refs[h][...] += dot1(yk_ref[h], ds_in[h], TN)
        g_store(h).start()
    total = own[...]
    for k in range(1, sections):
        cross(k).wait_recv()
        total = total + cross_in[k - 1].astype(F32)
    out_ref[...] = total.T.astype(BF16)
    out_store = pltpu.make_async_copy(out_ref, out_hbm, stored.at[heads])
    out_store.start()
    for k in range(sections):
        pair(k).wait_send()
        near(k).wait_send()
    for k in range(1, sections):
        cross(k).wait_send()
        far(k).wait_send()

    @pl.when(jnp.logical_not(last))
    def _():
        for h in range(heads):
            up(h).wait_send()

    @pl.when(jnp.logical_not(first))
    def _():
        for h in range(heads):
            down(h).wait_send()

    for h in range(heads):
        g_store(h).wait()
    out_store.wait()


PIECES = 4


def results_kernel(out_in, g_in, out_ref, g_ref, out_held, g_held, loaded, stored):
    rows = g_in.shape[0] // PIECES
    routes = [(out_in, out_held, out_ref)]
    for i in range(PIECES):
        part = pl.ds(i * rows, rows)
        routes.append((g_in.at[part], g_held.at[part], g_ref.at[part]))
    loads = [pltpu.make_async_copy(a, b, loaded.at[i]) for i, (a, b, _) in enumerate(routes)]
    stores = [pltpu.make_async_copy(b, c, stored.at[i]) for i, (_, b, c) in enumerate(routes)]
    for load in loads:
        load.start()
    for load, store in zip(loads, stores):
        load.wait()
        store.start()
    for store in stores:
        store.wait()


def per_device(queries, reflect_keys, reflect_values, reflect_betas, decay_rates, resets,
               out_weight, out_cotangent):
    tokens = queries.shape[0]
    heads = reflect_betas.shape[2]
    width = queries.shape[1] // heads
    steps = 2 * tokens
    devices = lax.axis_size("seq")
    sections = lax.axis_size("section")
    features = out_weight.shape[1] // (2 * sections)

    square = (heads, width, width)
    pairs = (heads, tokens, 2, width)
    vmem = pl.BlockSpec(memory_space=pltpu.VMEM)
    hbm = pl.BlockSpec(memory_space=pl.ANY)
    dma = pltpu.SemaphoreType.DMA
    shapes = [jax.ShapeDtypeStruct((features, tokens), BF16),
              jax.ShapeDtypeStruct((tokens, 2, heads * width), F32)]
    output, value_grads = pl.pallas_call(
        functools.partial(layer_kernel, devices, sections),
        in_specs=[vmem] * 3 + [hbm] * 5,
        out_specs=[hbm] * 2,
        out_shape=shapes,
        scratch_shapes=[pltpu.VMEM(queries.shape, BF16), pltpu.VMEM(pairs, BF16), pltpu.VMEM(pairs, BF16),
                        pltpu.VMEM(out_weight.shape, BF16), pltpu.VMEM((tokens, out_weight.shape[1]), BF16),
                        pltpu.VMEM(square, F32), pltpu.VMEM(square, F32),
                        pltpu.VMEM((heads, tokens, width), BF16), pltpu.VMEM((heads, tokens, width), F32),
                        pltpu.VMEM((heads, tokens, steps), BF16), pltpu.VMEM((heads, width, steps), BF16),
                        pltpu.VMEM(pairs, F32),
                        pltpu.VMEM((features, tokens), BF16)]
        + [pltpu.VMEM(square, BF16)] * 4
        + [pltpu.VMEM(square, F32), pltpu.VMEM((tokens, heads * width), BF16)]
        + [pltpu.VMEM((tokens, heads * width), BF16), pltpu.VMEM((tokens, features), F32),
           pltpu.VMEM((sections, tokens, features), F32),
           pltpu.VMEM((sections, tokens, features), F32),
           pltpu.VMEM((sections - 1, tokens, features), BF16),
           pltpu.VMEM((sections - 1, tokens, features), BF16)]
        + [dma((heads,)), dma((heads,)), dma((3,)), dma((heads + 1,))]
        + [dma((heads,))] * 4 + [dma((sections,))] * 2 + [dma((sections - 1,))] * 2
        + [dma((sections,))] * 2 + [dma((sections - 1,))] * 2,
        compiler_params=pltpu.CompilerParams(
            collective_id=0, has_side_effects=True, vmem_limit_bytes=58 << 20),
        name="layer",
    )(decay_rates.T, reflect_betas.transpose(1, 2, 0), resets.reshape(1, tokens),
      queries, reflect_keys, reflect_values, out_weight, out_cotangent)
    return pl.pallas_call(
        results_kernel,
        in_specs=[hbm] * 2,
        out_specs=[hbm] * 2,
        out_shape=shapes,
        scratch_shapes=[pltpu.VMEM(a.shape, a.dtype) for a in shapes] + [dma((PIECES + 1,))] * 2,
        compiler_params=pltpu.CompilerParams(vmem_limit_bytes=58 << 20),
        name="results",
    )(output, value_grads)


def solution(mesh):
    return jax.shard_map(
        per_device,
        mesh=mesh,
        in_specs=(
            P(("grp", "seq"), ("section", "head")),
            P(("grp", "seq"), None, ("section", "head")),
            P(("grp", "seq"), None, ("section", "head")),
            P(("grp", "seq"), None, ("section", "head")),
            P(("grp", "seq"), ("section", "head")),
            P(("grp", "seq")),
            P(("section", "head"), None),
            P(("grp", "seq"), ("section", "head")),
        ),
        out_specs=(
            P(("section", "head"), ("grp", "seq")),
            P(("grp", "seq"), None, ("section", "head")),
        ),
        check_vma=False,
    )
```

```python
import functools
import jax
import jax.numpy as jnp
from jax import lax
from jax.experimental import pallas as pl
from jax.experimental.pallas import tpu as pltpu
from jax.sharding import PartitionSpec as P

HALF = 64
BLK = 2 * HALF
F32 = jnp.float32
BF16 = jnp.bfloat16
NN = (((1,), (0,)), ((), ()))
NT = (((1,), (1,)), ((), ()))
TN = (((0,), (0,)), ((), ()))
MESH = pl.DeviceIdType.MESH


def dot1(a, b, dims=NN):
    return lax.dot_general(a.astype(BF16), b.astype(BF16), dims, preferred_element_type=F32)


def halves(a):
    high = a.astype(BF16)
    return high, (a - high.astype(F32)).astype(BF16)


def dot3(a, b, dims=NN):
    ah, al = halves(a)
    bh, bl = halves(b)
    n = b.shape[1]
    both = lax.dot_general(jnp.concatenate([ah, al], axis=1),
                           jnp.concatenate([jnp.concatenate([bh, bl], axis=1),
                                            jnp.concatenate([bh, jnp.zeros_like(bl)], axis=1)], axis=0),
                           dims, preferred_element_type=F32)
    return both[:, :n] + both[:, n:]


def thirds(a):
    top = a.astype(BF16)
    rest = a - top.astype(F32)
    middle = rest.astype(BF16)
    return jnp.concatenate([top, middle, (rest - middle.astype(F32)).astype(BF16)], axis=0)


def exact_dot(a, b):
    rows = a.shape[0]
    sums = dot1(thirds(a), b)
    return sums[:rows] + sums[rows:2 * rows] + sums[2 * rows:]


def iota(shape, axis):
    return lax.broadcasted_iota(jnp.int32, shape, axis)


def padded(parts, tokens):
    count = sum(p.shape[0] for p in parts)
    return jnp.concatenate(parts + [jnp.zeros((-count % 16, tokens), F32)], axis=0)


def schedules(decay, resets, betas):
    heads, tokens = decay.shape
    steps = 2 * tokens
    source, target = iota((tokens, 2 * tokens), 0), iota((tokens, 2 * tokens), 1)
    sums = exact_dot(padded([decay, resets], tokens), (source <= target) & (target < tokens)
                     | (source < target - tokens))
    inclusive, exclusive = sums[:, :tokens], sums[:, tokens:]
    even = padded([exclusive[:heads], inclusive[heads:heads + 1], betas[0]], tokens)
    odd = padded([inclusive[:heads + 1], betas[1]], tokens)
    source, target = iota((steps, steps), 0), iota((steps, steps), 1)
    spread = source == (target & 1) * tokens + (target >> 1)
    rows = exact_dot(jnp.concatenate([even, odd], axis=1), spread)
    return rows, rows.T, inclusive.T


def local(heads, schedule, q_ref, k_refs, v_refs, yq_ref, yk_ref, r_ref, m_ref, o_ref, b_ref):
    rows, cols, tok_cols = schedule
    tokens = q_ref.shape[0]
    width = m_ref.shape[1]
    blocks = tokens // HALF
    steps = 2 * tokens
    everything = [(h, b) for h in range(heads) for b in range(blocks)]
    z_row, z_col, z_tok = rows[heads:heads + 1], cols[:, heads:heads + 1], tok_cols[:, heads:heads + 1]
    c_row = [rows[h:h + 1] for h in range(heads)]
    c_col = [cols[:, h:h + 1] for h in range(heads)]
    c_tok = [tok_cols[:, h:h + 1] for h in range(heads)]
    beta_row = [rows[heads + 1 + h:heads + 2 + h] for h in range(heads)]
    beta_col = [cols[:, heads + 1 + h:heads + 2 + h] for h in range(heads)]
    z_end = z_row[:, steps - 1:]

    def sl(b):
        return slice(b * BLK, (b + 1) * BLK)

    def ts(b):
        return slice(b * HALF, (b + 1) * HALF)

    def lanes(h):
        return slice(h * width, (h + 1) * width)

    keys = {(h, b): k_refs[h][sl(b), :] for h, b in everything}
    tm_r, tm_c = iota((BLK, BLK), 0), iota((BLK, BLK), 1)
    eye = tm_r == tm_c
    identity = jnp.where(eye, 1.0, 0.0)

    low, scale_row, scale_col, gram = {}, {}, {}, {}
    for h, b in everything:
        for c in range(b + 1):
            gram[h, b, c] = dot1(keys[h, b], keys[h, c], NT)
    for h, b in everything:
        diag = jnp.where(eye, gram[h, b, b], 0.0)
        scale_row[h, b] = lax.rsqrt(jnp.sum(diag, axis=0, keepdims=True) + 1e-6)
        scale_col[h, b] = lax.rsqrt(jnp.sum(diag, axis=1, keepdims=True) + 1e-6)
    for h, b in everything:
        left = beta_col[h][sl(b)] * scale_col[h, b]
        for c in range(b + 1):
            valid = z_col[sl(b)] == z_row[:, sl(c)]
            if b == c:
                valid = valid & (tm_r > tm_c)
            gap = jnp.where(valid, c_row[h][:, sl(c)] - c_col[h][sl(b)], 0.0)
            low[h, b, c] = jnp.where(
                valid, jnp.exp(gap) * gram[h, b, c] * left * scale_row[h, c], 0.0)

    rounded = {i: low[i[0], i[1], i[1]].astype(BF16) for i in everything}
    inverse = {i: identity - jnp.where((tm_r >> 1) == (tm_c >> 1), low[i[0], i[1], i[1]], 0.0)
               for i in everything}
    level = 2
    while (1 << level) <= BLK:
        pick = ((tm_r >> level) == (tm_c >> level)) & ((tm_r >> (level - 1)) != (tm_c >> (level - 1)))
        narrow = {i: inverse[i].astype(BF16) for i in everything}
        inner = {i: dot1(jnp.where(pick, rounded[i], jnp.zeros_like(rounded[i])), narrow[i])
                 for i in everything}
        inverse = {i: inverse[i] - dot1(narrow[i], inner[i]) for i in everything}
        level += 1
    for _ in range(2):
        residual = {i: dot3(low[i[0], i[1], i[1]], inverse[i]) + (inverse[i] - identity)
                    for i in everything}
        inverse = {i: inverse[i] - dot1(inverse[i], residual[i]) for i in everything}
    gamma_row = [jnp.where(z_row == 0, jnp.exp(-c_row[h]), 0.0) for h in range(heads)]

    def solve(hs, right):
        solved = {}
        for b in reversed(range(blocks)):
            for h in hs:
                x = right(h, b)
                if b + 1 < blocks:
                    later = []
                    for c in range(b + 1, blocks):
                        short = x.shape[0] - solved[h, c].shape[0]
                        later.append(jnp.concatenate([jnp.zeros((short, BLK), F32), solved[h, c]], axis=0)
                                     if short else solved[h, c])
                    x = x - dot3(jnp.concatenate(later, axis=1),
                                 jnp.concatenate([low[h, c, b] for c in range(b + 1, blocks)], axis=0))
                solved[h, b] = dot3(x, inverse[h, b])
        return solved

    def products(h, solved, y_ref):
        plain, moved = [], []
        for b in range(blocks):
            y = solved[h, b] * beta_row[h][:, sl(b)]
            short = y_ref.shape[1] - y.shape[0]
            if short:
                y = jnp.concatenate([jnp.zeros((short, BLK), F32), y], axis=0)
            plain.append(y.astype(BF16))
            moved.append((y * (gamma_row[h][:, sl(b)] * scale_row[h, b])).astype(BF16))
            y_ref[h, :, sl(b)] = plain[b]
        return (dot1(jnp.concatenate(plain, axis=1), v_refs[h][...]),
                dot1(jnp.concatenate(moved, axis=1), k_refs[h][...]))

    gamma_end_row = [jnp.where(z_row == z_end, jnp.exp(c_row[h] - c_row[h][:, steps - 1:]), 0.0)
                     for h in range(heads)]

    def end_side(h, b):
        return keys[h, b].astype(F32).T * (scale_row[h, b] * gamma_end_row[h][:, sl(b)])

    def token_side(h, b):
        parts = []
        for a in range(b, blocks):
            product = dot1(q_ref[ts(a), lanes(h)], keys[h, b], NT)
            valid = z_tok[ts(a)] == z_row[:, sl(b)]
            if a == b:
                valid = valid & (iota((HALF, BLK), 0) >= (iota((HALF, BLK), 1) >> 1))
            gap = jnp.where(valid, c_row[h][:, sl(b)] - c_tok[h][ts(a)], 0.0)
            parts.append(jnp.where(valid, jnp.exp(gap) * product * scale_row[h, b], 0.0))
        return jnp.concatenate(parts, axis=0)

    def end_of(hs):
        solved = solve(hs, end_side)
        for h in hs:
            plain, moved = products(h, solved, yk_ref)
            gamma_end = jnp.where(z_end == 0, jnp.exp(-c_row[h][:, steps - 1:]), 0.0)
            b_ref[h] = plain
            m_ref[h] = jnp.where(iota((width, width), 0) == iota((width, width), 1), gamma_end, 0.0) - moved

    def tokens_of(hs):
        solved = solve(hs, token_side)
        for h in hs:
            plain, moved = products(h, solved, yq_ref)
            o_ref[h] = plain
            gamma_tok = jnp.where(z_tok == 0, jnp.exp(-c_tok[h]), 0.0)
            r_ref[h] = (gamma_tok * q_ref[:, lanes(h)].astype(F32) - moved).astype(BF16)

    return end_of, tokens_of


def layer_kernel(devices, sections, decay_ref, beta_ref, reset_ref, q_hbm, k_hbm, v_hbm, w_hbm, cot_hbm,
                 own_hbm, cross_in, g_hbm,
                 q_ref, k_ref, v_ref, w_ref, cot_ref, m_ref, b_ref, r_ref, o_ref, yq_ref, yk_ref, g_ref,
                 s_in, s_out, ds_in, ds_out, d, up_,
                 mixed, own, pair_out, pair_in, cross_out,
                 k_loaded, v_loaded, loaded, stored,
                 s_sent, s_got, ds_sent, ds_got, pair_sent, pair_got, cross_sent, cross_got,
                 near_sent, near_got, far_sent, far_got):
    heads, tokens, width = r_ref.shape
    features = own.shape[1]
    share = cot_hbm.shape[1]
    place = lax.axis_index("seq")
    section, core = lax.axis_index("section"), lax.axis_index("head")
    sibling = 1 - core
    first, last = place == 0, place == devices - 1

    def peer(k):
        return lax.rem(section + k, sections)

    def owned(part, side):
        return pl.ds(pl.multiple_of((part * 2 + side) * share, 128), share)

    barrier = pltpu.get_barrier_semaphore()

    @pl.when(jnp.logical_not(first))
    def _():
        pl.semaphore_signal(barrier, inc=1, device_id={"seq": place - 1}, device_id_type=MESH)

    @pl.when(jnp.logical_not(last))
    def _():
        pl.semaphore_signal(barrier, inc=1, device_id={"seq": place + 1}, device_id_type=MESH)

    pl.semaphore_signal(barrier, inc=1, device_id={"head": sibling}, device_id_type=MESH)
    for k in range(1, sections):
        pl.semaphore_signal(barrier, inc=1, device_id={"section": peer(k)}, device_id_type=MESH)

    def strip(h):
        return pl.ds(h * width, width)

    k_loads = [pltpu.make_async_copy(k_hbm.at[:, :, strip(h)], k_ref.at[h], k_loaded.at[h]) for h in range(heads)]
    v_loads = [pltpu.make_async_copy(v_hbm.at[:, :, strip(h)], v_ref.at[h], v_loaded.at[h]) for h in range(heads)]
    q_load = pltpu.make_async_copy(q_hbm, q_ref, loaded.at[0])
    w_load = pltpu.make_async_copy(w_hbm, w_ref, loaded.at[1])
    cot_load = pltpu.make_async_copy(cot_hbm, cot_ref.at[:, owned(section, core)], loaded.at[2])
    for load in k_loads + v_loads + [q_load, cot_load, w_load]:
        load.start()

    def far(k):
        return pltpu.make_async_remote_copy(
            src_ref=cot_hbm, dst_ref=cot_ref.at[:, owned(section, core)],
            send_sem=far_sent.at[k - 1], recv_sem=far_got.at[k - 1],
            device_id={"section": peer(k)}, device_id_type=MESH)

    def near(k):
        block = owned(peer(sections - k), core)
        return pltpu.make_async_remote_copy(
            src_ref=cot_ref.at[:, block] if k else cot_hbm, dst_ref=cot_ref.at[:, block],
            send_sem=near_sent.at[k], recv_sem=near_got.at[k],
            device_id={"head": sibling}, device_id_type=MESH)

    schedule = schedules(decay_ref[...], reset_ref[...].astype(F32), beta_ref[...])
    pl.semaphore_wait(barrier, sections + jnp.where(first, 0, 1) + jnp.where(last, 0, 1))
    for k in range(1, sections):
        far(k).start()
    near(0).start()
    k_refs = [k_ref.at[h].reshape(2 * tokens, width) for h in range(heads)]
    v_refs = [v_ref.at[h].reshape(2 * tokens, width) for h in range(heads)]

    def up(h):
        return pltpu.make_async_remote_copy(
            src_ref=s_out.at[h], dst_ref=s_in.at[h], send_sem=s_sent.at[h], recv_sem=s_got.at[h],
            device_id={"seq": place + 1}, device_id_type=MESH)

    def down(h):
        return pltpu.make_async_remote_copy(
            src_ref=ds_out.at[h], dst_ref=ds_in.at[h], send_sem=ds_sent.at[h], recv_sem=ds_got.at[h],
            device_id={"seq": place - 1}, device_id_type=MESH)

    def forward():
        for h in range(heads):
            up(h).wait_recv()

            @pl.when(jnp.logical_not(last))
            def _():
                s = s_in[h]
                mh, ml = halves(m_ref[h])
                s_out[h] = (dot1(mh, s) + dot1(ml, s) + b_ref[h]).astype(BF16)
                up(h).start()

    def backward():
        for h in range(heads):
            down(h).wait_recv()

            @pl.when(jnp.logical_not(first))
            def _():
                ds = ds_in[h]
                mh, ml = halves(m_ref[h])
                ds_out[h] = (dot1(mh, ds, TN) + dot1(ml, ds, TN) + d[h]).astype(BF16)
                down(h).start()

    def relay():
        for k in range(1, sections):
            far(k).wait_recv()
            near(k).start()

    for load in k_loads:
        load.wait()
    end_of, tokens_of = local(heads, schedule, q_ref, k_refs, v_refs, yq_ref, yk_ref, r_ref, m_ref, o_ref, b_ref)
    for load in v_loads + [q_load]:
        load.wait()

    @pl.when(jnp.logical_not(last))
    def _():
        end_of(range(heads))

    @pl.when(first)
    def _():
        for h in range(heads):
            s_in[h] = jnp.zeros(s_in.shape[1:], BF16)
            s_out[h] = b_ref[h].astype(BF16)
            up(h).start()

    relay()
    tokens_of(range(heads // 2))
    w_load.wait()
    cot_load.wait()
    for k in range(sections):
        near(k).wait_recv()
    up_[...] = dot1(cot_ref[...], w_ref[...], NT).astype(BF16)

    @pl.when(place == 1)
    def _():
        forward()

    tokens_of(range(heads // 2, heads))
    for h in range(heads):
        d[h] = dot1(r_ref[h], up_[:, strip(h)], TN)
    high = 2 * place >= devices

    @pl.when(last)
    def _():
        for h in range(heads):
            ds_out[h] = d[h].astype(BF16)
            down(h).start()

    @pl.when(jnp.logical_and(high, jnp.logical_not(last)))
    def _():
        backward()

    @pl.when(place > 1)
    def _():
        forward()

    for h in range(heads):
        mixed[:, strip(h)] = (dot1(r_ref[h], s_in[h]) + o_ref[h]).astype(BF16)

    def partial(target, side):
        start = pl.multiple_of((target * 2 + side) * features, 128)
        return dot1(mixed[...], w_ref[:, pl.ds(start, features)])

    def pair(k):
        return pltpu.make_async_remote_copy(
            src_ref=pair_out.at[k], dst_ref=pair_in.at[k], send_sem=pair_sent.at[k],
            recv_sem=pair_got.at[k], device_id={"head": sibling}, device_id_type=MESH)

    def cross(k):
        return pltpu.make_async_remote_copy(
            src_ref=cross_out.at[k - 1], dst_ref=cross_in.at[k - 1], send_sem=cross_sent.at[k - 1],
            recv_sem=cross_got.at[k - 1], device_id={"section": peer(k)}, device_id_type=MESH)

    for k in range(1, sections):
        pair_out[k] = partial(peer(k), sibling)
        pair(k).start()
    for k in range(1, sections):
        mine = partial(peer(k), core)
        pair(k).wait_recv()
        cross_out[k - 1] = (mine + pair_in[k]).astype(BF16)
        cross(k).start()
    pair_out[0] = partial(section, sibling)
    pair(0).start()

    def g_store(h):
        return pltpu.make_async_copy(g_ref.at[h], g_hbm.at[:, :, strip(h)], stored.at[h])

    g_refs = [g_ref.at[h].reshape(2 * tokens, width) for h in range(heads)]
    for h in range(heads):
        g_refs[h][...] = dot1(yq_ref[h], up_[:, strip(h)], TN)
    total = partial(section, core)
    pair(0).wait_recv()
    own[...] = total + pair_in[0]
    own_store = pltpu.make_async_copy(own, own_hbm, stored.at[heads])
    own_store.start()

    @pl.when(jnp.logical_not(high))
    def _():
        backward()

    for h in range(heads):
        @pl.when(jnp.logical_not(last))
        def _():
            g_refs[h][...] += dot1(yk_ref[h], ds_in[h], TN)

        g_store(h).start()
    for k in range(1, sections):
        cross(k).wait_recv()
    for k in range(sections):
        pair(k).wait_send()
        near(k).wait_send()
    for k in range(1, sections):
        cross(k).wait_send()
        far(k).wait_send()

    @pl.when(jnp.logical_not(last))
    def _():
        for h in range(heads):
            up(h).wait_send()

    @pl.when(jnp.logical_not(first))
    def _():
        for h in range(heads):
            down(h).wait_send()

    for h in range(heads):
        g_store(h).wait()
    own_store.wait()


def results_kernel(own_hbm, cross_hbm, g_hbm, out_hbm, grads_hbm, own, cross, g, out, loaded, stored):
    pieces = loaded.shape[0] - 2
    rows = g.shape[0] // pieces
    parts = [pl.ds(i * rows, rows) for i in range(pieces)]
    loads = [pltpu.make_async_copy(own_hbm, own, loaded.at[0]), pltpu.make_async_copy(cross_hbm, cross, loaded.at[1])]
    loads += [pltpu.make_async_copy(g_hbm.at[p], g.at[p], loaded.at[2 + i]) for i, p in enumerate(parts)]
    stores = [pltpu.make_async_copy(out, out_hbm, stored.at[0])]
    stores += [pltpu.make_async_copy(g.at[p], grads_hbm.at[p], stored.at[1 + i]) for i, p in enumerate(parts)]
    for load in loads:
        load.start()
    loads[0].wait()
    loads[1].wait()
    total = own[...]
    for k in range(cross.shape[0]):
        total = total + cross[k].astype(F32)
    out[...] = total.T.astype(BF16)
    stores[0].start()
    for load, store in zip(loads[2:], stores[1:]):
        load.wait()
        store.start()
    for store in stores:
        store.wait()


PIECES = 4


def per_device(queries, reflect_keys, reflect_values, reflect_betas, decay_rates, resets,
               out_weight, out_cotangent):
    tokens = queries.shape[0]
    heads = reflect_betas.shape[2]
    width = queries.shape[1] // heads
    steps = 2 * tokens
    devices = lax.axis_size("seq")
    sections = lax.axis_size("section")
    features = out_weight.shape[1] // (2 * sections)

    square = (heads, width, width)
    pairs = (heads, tokens, 2, width)
    vmem = pl.BlockSpec(memory_space=pltpu.VMEM)
    hbm = pl.BlockSpec(memory_space=pl.ANY)
    dma = pltpu.SemaphoreType.DMA
    shapes = [jax.ShapeDtypeStruct((features, tokens), BF16),
              jax.ShapeDtypeStruct((tokens, 2, heads * width), F32)]
    parts = [jax.ShapeDtypeStruct((tokens, features), F32),
             jax.ShapeDtypeStruct((sections - 1, tokens, features), BF16), shapes[1]]
    own, cross, grads = pl.pallas_call(
        functools.partial(layer_kernel, devices, sections),
        in_specs=[vmem] * 3 + [hbm] * 5,
        out_specs=[hbm] * 3,
        out_shape=parts,
        scratch_shapes=[pltpu.VMEM(queries.shape, BF16), pltpu.VMEM(pairs, BF16), pltpu.VMEM(pairs, BF16),
                        pltpu.VMEM(out_weight.shape, BF16), pltpu.VMEM((tokens, out_weight.shape[1]), BF16),
                        pltpu.VMEM(square, F32), pltpu.VMEM(square, F32),
                        pltpu.VMEM((heads, tokens, width), BF16), pltpu.VMEM((heads, tokens, width), F32),
                        pltpu.VMEM((heads, tokens, steps), BF16), pltpu.VMEM((heads, width, steps), BF16),
                        pltpu.VMEM(pairs, F32)]
        + [pltpu.VMEM(square, BF16)] * 4
        + [pltpu.VMEM(square, F32), pltpu.VMEM((tokens, heads * width), BF16)]
        + [pltpu.VMEM((tokens, heads * width), BF16), pltpu.VMEM((tokens, features), F32),
           pltpu.VMEM((sections, tokens, features), F32),
           pltpu.VMEM((sections, tokens, features), F32),
           pltpu.VMEM((sections - 1, tokens, features), BF16)]
        + [dma((heads,)), dma((heads,)), dma((3,)), dma((heads + 1,))]
        + [dma((heads,))] * 4 + [dma((sections,))] * 2 + [dma((sections - 1,))] * 2
        + [dma((sections,))] * 2 + [dma((sections - 1,))] * 2,
        compiler_params=pltpu.CompilerParams(
            collective_id=0, has_side_effects=True, vmem_limit_bytes=58 << 20),
        name="layer",
    )(decay_rates.T, reflect_betas.transpose(1, 2, 0), resets.reshape(1, tokens),
      queries, reflect_keys, reflect_values, out_weight, out_cotangent)
    return pl.pallas_call(
        results_kernel,
        in_specs=[hbm] * 3,
        out_specs=[hbm] * 2,
        out_shape=shapes,
        scratch_shapes=[pltpu.VMEM(a.shape, a.dtype) for a in parts] + [pltpu.VMEM(shapes[0].shape, BF16)]
        + [dma((PIECES + 2,)), dma((PIECES + 1,))],
        compiler_params=pltpu.CompilerParams(vmem_limit_bytes=58 << 20),
        name="results",
    )(own, cross, grads)


def solution(mesh):
    return jax.shard_map(
        per_device,
        mesh=mesh,
        in_specs=(
            P(("grp", "seq"), ("section", "head")),
            P(("grp", "seq"), None, ("section", "head")),
            P(("grp", "seq"), None, ("section", "head")),
            P(("grp", "seq"), None, ("section", "head")),
            P(("grp", "seq"), ("section", "head")),
            P(("grp", "seq")),
            P(("section", "head"), None),
            P(("grp", "seq"), ("section", "head")),
        ),
        out_specs=(
            P(("section", "head"), ("grp", "seq")),
            P(("grp", "seq"), None, ("section", "head")),
        ),
        check_vma=False,
    )
```

```python
import functools
import jax
import jax.numpy as jnp
from jax import lax
from jax.experimental import pallas as pl
from jax.experimental.pallas import tpu as pltpu
from jax.sharding import PartitionSpec as P

HALF = 64
BLK = 2 * HALF
F32 = jnp.float32
BF16 = jnp.bfloat16
NN = (((1,), (0,)), ((), ()))
NT = (((1,), (1,)), ((), ()))
TN = (((0,), (0,)), ((), ()))
MESH = pl.DeviceIdType.MESH


def dot1(a, b, dims=NN):
    return lax.dot_general(a.astype(BF16), b.astype(BF16), dims, preferred_element_type=F32)


def halves(a):
    high = a.astype(BF16)
    return high, (a - high.astype(F32)).astype(BF16)


def dot3(a, b, dims=NN):
    ah, al = halves(a)
    bh, bl = halves(b)
    n = b.shape[1]
    both = lax.dot_general(jnp.concatenate([ah, al], axis=1),
                           jnp.concatenate([jnp.concatenate([bh, bl], axis=1),
                                            jnp.concatenate([bh, jnp.zeros_like(bl)], axis=1)], axis=0),
                           dims, preferred_element_type=F32)
    return both[:, :n] + both[:, n:]


def thirds(a):
    top = a.astype(BF16)
    rest = a - top.astype(F32)
    middle = rest.astype(BF16)
    return jnp.concatenate([top, middle, (rest - middle.astype(F32)).astype(BF16)], axis=0)


def exact_dot(a, b):
    rows = a.shape[0]
    sums = dot1(thirds(a), b)
    return sums[:rows] + sums[rows:2 * rows] + sums[2 * rows:]


def iota(shape, axis):
    return lax.broadcasted_iota(jnp.int32, shape, axis)


def padded(parts, tokens):
    count = sum(p.shape[0] for p in parts)
    return jnp.concatenate(parts + [jnp.zeros((-count % 16, tokens), F32)], axis=0)


def schedules(decay, resets, betas):
    heads, tokens = decay.shape
    steps = 2 * tokens
    source, target = iota((tokens, 2 * tokens), 0), iota((tokens, 2 * tokens), 1)
    sums = exact_dot(padded([decay, resets], tokens), (source <= target) & (target < tokens)
                     | (source < target - tokens))
    inclusive, exclusive = sums[:, :tokens], sums[:, tokens:]
    even = padded([exclusive[:heads], inclusive[heads:heads + 1], betas[0]], tokens)
    odd = padded([inclusive[:heads + 1], betas[1]], tokens)
    source, target = iota((steps, steps), 0), iota((steps, steps), 1)
    spread = source == (target & 1) * tokens + (target >> 1)
    rows = exact_dot(jnp.concatenate([even, odd], axis=1), spread)
    return rows, rows.T, inclusive.T


def local(heads, schedule, q_ref, k_refs, v_refs, yq_ref, yk_ref, r_ref, m_ref, o_ref, b_ref):
    rows, cols, tok_cols = schedule
    tokens = q_ref.shape[0]
    width = m_ref.shape[1]
    blocks = tokens // HALF
    steps = 2 * tokens
    everything = [(h, b) for h in range(heads) for b in range(blocks)]
    z_row, z_col, z_tok = rows[heads:heads + 1], cols[:, heads:heads + 1], tok_cols[:, heads:heads + 1]
    c_row = [rows[h:h + 1] for h in range(heads)]
    c_col = [cols[:, h:h + 1] for h in range(heads)]
    c_tok = [tok_cols[:, h:h + 1] for h in range(heads)]
    beta_row = [rows[heads + 1 + h:heads + 2 + h] for h in range(heads)]
    beta_col = [cols[:, heads + 1 + h:heads + 2 + h] for h in range(heads)]
    z_end = z_row[:, steps - 1:]

    def sl(b):
        return slice(b * BLK, (b + 1) * BLK)

    def ts(b):
        return slice(b * HALF, (b + 1) * HALF)

    def lanes(h):
        return slice(h * width, (h + 1) * width)

    keys = {(h, b): k_refs[h][sl(b), :] for h, b in everything}
    tm_r, tm_c = iota((BLK, BLK), 0), iota((BLK, BLK), 1)
    eye = tm_r == tm_c
    identity = jnp.where(eye, 1.0, 0.0)

    low, scale_row, scale_col, gram = {}, {}, {}, {}
    for h, b in everything:
        for c in range(b + 1):
            gram[h, b, c] = dot1(keys[h, b], keys[h, c], NT)
    for h, b in everything:
        diag = jnp.where(eye, gram[h, b, b], 0.0)
        scale_row[h, b] = lax.rsqrt(jnp.sum(diag, axis=0, keepdims=True) + 1e-6)
        scale_col[h, b] = lax.rsqrt(jnp.sum(diag, axis=1, keepdims=True) + 1e-6)
    for h, b in everything:
        left = beta_col[h][sl(b)] * scale_col[h, b]
        for c in range(b + 1):
            valid = z_col[sl(b)] == z_row[:, sl(c)]
            if b == c:
                valid = valid & (tm_r > tm_c)
            gap = jnp.where(valid, c_row[h][:, sl(c)] - c_col[h][sl(b)], 0.0)
            low[h, b, c] = jnp.where(
                valid, jnp.exp(gap) * gram[h, b, c] * left * scale_row[h, c], 0.0)

    rounded = {i: low[i[0], i[1], i[1]].astype(BF16) for i in everything}
    inverse = {i: identity - jnp.where((tm_r >> 1) == (tm_c >> 1), low[i[0], i[1], i[1]], 0.0)
               for i in everything}
    level = 2
    while (1 << level) <= BLK:
        pick = ((tm_r >> level) == (tm_c >> level)) & ((tm_r >> (level - 1)) != (tm_c >> (level - 1)))
        narrow = {i: inverse[i].astype(BF16) for i in everything}
        inner = {i: dot1(jnp.where(pick, rounded[i], jnp.zeros_like(rounded[i])), narrow[i])
                 for i in everything}
        inverse = {i: inverse[i] - dot1(narrow[i], inner[i]) for i in everything}
        level += 1
    for _ in range(2):
        residual = {i: dot3(low[i[0], i[1], i[1]], inverse[i]) + (inverse[i] - identity)
                    for i in everything}
        inverse = {i: inverse[i] - dot1(inverse[i], residual[i]) for i in everything}
    gamma_row = [jnp.where(z_row == 0, jnp.exp(-c_row[h]), 0.0) for h in range(heads)]

    def solve(hs, right):
        solved = {}
        for b in reversed(range(blocks)):
            for h in hs:
                x = right(h, b)
                if b + 1 < blocks:
                    later = []
                    for c in range(b + 1, blocks):
                        short = x.shape[0] - solved[h, c].shape[0]
                        later.append(jnp.concatenate([jnp.zeros((short, BLK), F32), solved[h, c]], axis=0)
                                     if short else solved[h, c])
                    x = x - dot3(jnp.concatenate(later, axis=1),
                                 jnp.concatenate([low[h, c, b] for c in range(b + 1, blocks)], axis=0))
                solved[h, b] = dot3(x, inverse[h, b])
        return solved

    def products(h, solved, y_ref):
        plain, moved = [], []
        for b in range(blocks):
            y = solved[h, b] * beta_row[h][:, sl(b)]
            short = y_ref.shape[1] - y.shape[0]
            if short:
                y = jnp.concatenate([jnp.zeros((short, BLK), F32), y], axis=0)
            plain.append(y.astype(BF16))
            moved.append((y * (gamma_row[h][:, sl(b)] * scale_row[h, b])).astype(BF16))
            y_ref[h, :, sl(b)] = plain[b]
        return (dot1(jnp.concatenate(plain, axis=1), v_refs[h][...]),
                dot1(jnp.concatenate(moved, axis=1), k_refs[h][...]))

    gamma_end_row = [jnp.where(z_row == z_end, jnp.exp(c_row[h] - c_row[h][:, steps - 1:]), 0.0)
                     for h in range(heads)]

    def end_side(h, b):
        return keys[h, b].astype(F32).T * (scale_row[h, b] * gamma_end_row[h][:, sl(b)])

    def token_side(h, b):
        parts = []
        for a in range(b, blocks):
            product = dot1(q_ref[ts(a), lanes(h)], keys[h, b], NT)
            valid = z_tok[ts(a)] == z_row[:, sl(b)]
            if a == b:
                valid = valid & (iota((HALF, BLK), 0) >= (iota((HALF, BLK), 1) >> 1))
            gap = jnp.where(valid, c_row[h][:, sl(b)] - c_tok[h][ts(a)], 0.0)
            parts.append(jnp.where(valid, jnp.exp(gap) * product * scale_row[h, b], 0.0))
        return jnp.concatenate(parts, axis=0)

    def end_of(hs):
        solved = solve(hs, end_side)
        for h in hs:
            plain, moved = products(h, solved, yk_ref)
            gamma_end = jnp.where(z_end == 0, jnp.exp(-c_row[h][:, steps - 1:]), 0.0)
            b_ref[h] = plain
            m_ref[h] = jnp.where(iota((width, width), 0) == iota((width, width), 1), gamma_end, 0.0) - moved

    def tokens_of(hs):
        solved = solve(hs, token_side)
        for h in hs:
            plain, moved = products(h, solved, yq_ref)
            o_ref[h] = plain
            gamma_tok = jnp.where(z_tok == 0, jnp.exp(-c_tok[h]), 0.0)
            r_ref[h] = (gamma_tok * q_ref[:, lanes(h)].astype(F32) - moved).astype(BF16)

    return end_of, tokens_of


def layer_kernel(devices, sections, decay_ref, beta_ref, reset_ref, q_hbm, k_hbm, v_hbm, w_hbm, cot_hbm,
                 own_hbm, cross_in, g_hbm,
                 q_ref, k_ref, v_ref, w_ref, cot_ref, m_ref, b_ref, r_ref, o_ref, yq_ref, yk_ref, g_ref,
                 s_in, s_out, ds_in, ds_out, d, up_,
                 mixed, own, pair_out, pair_in, cross_out,
                 k_loaded, v_loaded, loaded, stored,
                 s_sent, s_got, ds_sent, ds_got, pair_sent, pair_got, cross_sent, cross_got,
                 near_sent, near_got, far_sent, far_got):
    heads, tokens, width = r_ref.shape
    features = own.shape[1]
    share = cot_hbm.shape[1]
    place = lax.axis_index("seq")
    section, core = lax.axis_index("section"), lax.axis_index("head")
    sibling = 1 - core
    first, last = place == 0, place == devices - 1

    def peer(k):
        return lax.rem(section + k, sections)

    def owned(part, side):
        return pl.ds(pl.multiple_of((part * 2 + side) * share, 128), share)

    barrier = pltpu.get_barrier_semaphore()

    @pl.when(jnp.logical_not(first))
    def _():
        pl.semaphore_signal(barrier, inc=1, device_id={"seq": place - 1}, device_id_type=MESH)

    @pl.when(jnp.logical_not(last))
    def _():
        pl.semaphore_signal(barrier, inc=1, device_id={"seq": place + 1}, device_id_type=MESH)

    pl.semaphore_signal(barrier, inc=1, device_id={"head": sibling}, device_id_type=MESH)
    for k in range(1, sections):
        pl.semaphore_signal(barrier, inc=1, device_id={"section": peer(k)}, device_id_type=MESH)

    def strip(h):
        return pl.ds(h * width, width)

    k_loads = [pltpu.make_async_copy(k_hbm.at[:, :, strip(h)], k_ref.at[h], k_loaded.at[h]) for h in range(heads)]
    v_loads = [pltpu.make_async_copy(v_hbm.at[:, :, strip(h)], v_ref.at[h], v_loaded.at[h]) for h in range(heads)]
    q_load = pltpu.make_async_copy(q_hbm, q_ref, loaded.at[0])
    w_load = pltpu.make_async_copy(w_hbm, w_ref, loaded.at[1])
    cot_load = pltpu.make_async_copy(cot_hbm, cot_ref.at[:, owned(section, core)], loaded.at[2])
    for load in k_loads + v_loads + [q_load, cot_load, w_load]:
        load.start()

    def far(k):
        return pltpu.make_async_remote_copy(
            src_ref=cot_hbm, dst_ref=cot_ref.at[:, owned(section, core)],
            send_sem=far_sent.at[k - 1], recv_sem=far_got.at[k - 1],
            device_id={"section": peer(k)}, device_id_type=MESH)

    def near(k):
        block = owned(peer(sections - k), core)
        return pltpu.make_async_remote_copy(
            src_ref=cot_ref.at[:, block] if k else cot_hbm, dst_ref=cot_ref.at[:, block],
            send_sem=near_sent.at[k], recv_sem=near_got.at[k],
            device_id={"head": sibling}, device_id_type=MESH)

    schedule = schedules(decay_ref[...], reset_ref[...].astype(F32), beta_ref[...])
    pl.semaphore_wait(barrier, sections + jnp.where(first, 0, 1) + jnp.where(last, 0, 1))
    for k in range(1, sections):
        far(k).start()
    near(0).start()
    k_refs = [k_ref.at[h].reshape(2 * tokens, width) for h in range(heads)]
    v_refs = [v_ref.at[h].reshape(2 * tokens, width) for h in range(heads)]

    def up(h):
        return pltpu.make_async_remote_copy(
            src_ref=s_out.at[h], dst_ref=s_in.at[h], send_sem=s_sent.at[h], recv_sem=s_got.at[h],
            device_id={"seq": place + 1}, device_id_type=MESH)

    def down(h):
        return pltpu.make_async_remote_copy(
            src_ref=ds_out.at[h], dst_ref=ds_in.at[h], send_sem=ds_sent.at[h], recv_sem=ds_got.at[h],
            device_id={"seq": place - 1}, device_id_type=MESH)

    def forward():
        for h in range(heads):
            up(h).wait_recv()

            @pl.when(jnp.logical_not(last))
            def _():
                s = s_in[h]
                mh, ml = halves(m_ref[h])
                s_out[h] = (dot1(mh, s) + dot1(ml, s) + b_ref[h]).astype(BF16)
                up(h).start()

    def backward():
        for h in range(heads):
            down(h).wait_recv()

            @pl.when(jnp.logical_not(first))
            def _():
                ds = ds_in[h]
                mh, ml = halves(m_ref[h])
                ds_out[h] = (dot1(mh, ds, TN) + dot1(ml, ds, TN) + d[h]).astype(BF16)
                down(h).start()

    def relay():
        for k in range(1, sections):
            far(k).wait_recv()
            near(k).start()

    for load in k_loads:
        load.wait()
    end_of, tokens_of = local(heads, schedule, q_ref, k_refs, v_refs, yq_ref, yk_ref, r_ref, m_ref, o_ref, b_ref)
    for load in v_loads + [q_load]:
        load.wait()

    parts = [range(heads // 2), range(heads // 2, heads)]
    for hs in [range(heads)]:
        @pl.when(jnp.logical_not(last))
        def _():
            end_of(hs)

        @pl.when(first)
        def _():
            for h in hs:
                s_in[h] = jnp.zeros(s_in.shape[1:], BF16)
                s_out[h] = b_ref[h].astype(BF16)
                up(h).start()

    tokens_of(parts[0])
    relay()

    @pl.when(place == 1)
    def _():
        forward()

    tokens_of(parts[1])
    w_load.wait()
    cot_load.wait()
    for k in range(sections):
        near(k).wait_recv()
    up_[...] = dot1(cot_ref[...], w_ref[...], NT).astype(BF16)
    for h in range(heads):
        d[h] = dot1(r_ref[h], up_[:, strip(h)], TN)
    high, middle = 2 * place > devices, 2 * place == devices

    @pl.when(last)
    def _():
        for h in range(heads):
            ds_out[h] = d[h].astype(BF16)
            down(h).start()

    @pl.when(jnp.logical_and(high, jnp.logical_not(last)))
    def _():
        backward()

    @pl.when(place > 1)
    def _():
        forward()

    @pl.when(middle)
    def _():
        backward()

    for h in range(heads):
        mixed[:, strip(h)] = (dot1(r_ref[h], s_in[h]) + o_ref[h]).astype(BF16)

    def partial(target, side):
        start = pl.multiple_of((target * 2 + side) * features, 128)
        return dot1(mixed[...], w_ref[:, pl.ds(start, features)])

    def pair(k):
        return pltpu.make_async_remote_copy(
            src_ref=pair_out.at[k], dst_ref=pair_in.at[k], send_sem=pair_sent.at[k],
            recv_sem=pair_got.at[k], device_id={"head": sibling}, device_id_type=MESH)

    def cross(k):
        return pltpu.make_async_remote_copy(
            src_ref=cross_out.at[k - 1], dst_ref=cross_in.at[k - 1], send_sem=cross_sent.at[k - 1],
            recv_sem=cross_got.at[k - 1], device_id={"section": peer(k)}, device_id_type=MESH)

    for k in range(1, sections):
        pair_out[k] = partial(peer(k), sibling)
        pair(k).start()
    for k in range(1, sections):
        mine = partial(peer(k), core)
        pair(k).wait_recv()
        cross_out[k - 1] = (mine + pair_in[k]).astype(BF16)
        cross(k).start()
    pair_out[0] = partial(section, sibling)
    pair(0).start()

    def g_store(h):
        return pltpu.make_async_copy(g_ref.at[h], g_hbm.at[:, :, strip(h)], stored.at[h])

    g_refs = [g_ref.at[h].reshape(2 * tokens, width) for h in range(heads)]
    for h in range(heads):
        g_refs[h][...] = dot1(yq_ref[h], up_[:, strip(h)], TN)
    total = partial(section, core)
    pair(0).wait_recv()
    own[...] = total + pair_in[0]
    own_store = pltpu.make_async_copy(own, own_hbm, stored.at[heads])
    own_store.start()

    @pl.when(2 * place < devices)
    def _():
        backward()

    for h in range(heads):
        @pl.when(jnp.logical_not(last))
        def _():
            g_refs[h][...] += dot1(yk_ref[h], ds_in[h], TN)

        g_store(h).start()
    for k in range(1, sections):
        cross(k).wait_recv()
    for k in range(sections):
        pair(k).wait_send()
        near(k).wait_send()
    for k in range(1, sections):
        cross(k).wait_send()
        far(k).wait_send()

    @pl.when(jnp.logical_not(last))
    def _():
        for h in range(heads):
            up(h).wait_send()

    @pl.when(jnp.logical_not(first))
    def _():
        for h in range(heads):
            down(h).wait_send()

    for h in range(heads):
        g_store(h).wait()
    own_store.wait()


def results_kernel(own_hbm, cross_hbm, g_hbm, out_hbm, grads_hbm, own, cross, g, out, loaded, stored):
    pieces = loaded.shape[0] - 2
    rows = g.shape[0] // pieces
    parts = [pl.ds(i * rows, rows) for i in range(pieces)]
    loads = [pltpu.make_async_copy(own_hbm, own, loaded.at[0]), pltpu.make_async_copy(cross_hbm, cross, loaded.at[1])]
    loads += [pltpu.make_async_copy(g_hbm.at[p], g.at[p], loaded.at[2 + i]) for i, p in enumerate(parts)]
    stores = [pltpu.make_async_copy(out, out_hbm, stored.at[0])]
    stores += [pltpu.make_async_copy(g.at[p], grads_hbm.at[p], stored.at[1 + i]) for i, p in enumerate(parts)]
    for load in loads:
        load.start()
    loads[0].wait()
    loads[1].wait()
    total = own[...]
    for k in range(cross.shape[0]):
        total = total + cross[k].astype(F32)
    out[...] = total.T.astype(BF16)
    stores[0].start()
    for load, store in zip(loads[2:], stores[1:]):
        load.wait()
        store.start()
    for store in stores:
        store.wait()


PIECES = 4


def per_device(queries, reflect_keys, reflect_values, reflect_betas, decay_rates, resets,
               out_weight, out_cotangent):
    tokens = queries.shape[0]
    heads = reflect_betas.shape[2]
    width = queries.shape[1] // heads
    steps = 2 * tokens
    devices = lax.axis_size("seq")
    sections = lax.axis_size("section")
    features = out_weight.shape[1] // (2 * sections)

    square = (heads, width, width)
    pairs = (heads, tokens, 2, width)
    vmem = pl.BlockSpec(memory_space=pltpu.VMEM)
    hbm = pl.BlockSpec(memory_space=pl.ANY)
    dma = pltpu.SemaphoreType.DMA
    shapes = [jax.ShapeDtypeStruct((features, tokens), BF16),
              jax.ShapeDtypeStruct((tokens, 2, heads * width), F32)]
    parts = [jax.ShapeDtypeStruct((tokens, features), F32),
             jax.ShapeDtypeStruct((sections - 1, tokens, features), BF16), shapes[1]]
    own, cross, grads = pl.pallas_call(
        functools.partial(layer_kernel, devices, sections),
        in_specs=[vmem] * 3 + [hbm] * 5,
        out_specs=[hbm] * 3,
        out_shape=parts,
        scratch_shapes=[pltpu.VMEM(queries.shape, BF16), pltpu.VMEM(pairs, BF16), pltpu.VMEM(pairs, BF16),
                        pltpu.VMEM(out_weight.shape, BF16), pltpu.VMEM((tokens, out_weight.shape[1]), BF16),
                        pltpu.VMEM(square, F32), pltpu.VMEM(square, F32),
                        pltpu.VMEM((heads, tokens, width), BF16), pltpu.VMEM((heads, tokens, width), F32),
                        pltpu.VMEM((heads, tokens, steps), BF16), pltpu.VMEM((heads, width, steps), BF16),
                        pltpu.VMEM(pairs, F32)]
        + [pltpu.VMEM(square, BF16)] * 4
        + [pltpu.VMEM(square, F32), pltpu.VMEM((tokens, heads * width), BF16)]
        + [pltpu.VMEM((tokens, heads * width), BF16), pltpu.VMEM((tokens, features), F32),
           pltpu.VMEM((sections, tokens, features), F32),
           pltpu.VMEM((sections, tokens, features), F32),
           pltpu.VMEM((sections - 1, tokens, features), BF16)]
        + [dma((heads,)), dma((heads,)), dma((3,)), dma((heads + 1,))]
        + [dma((heads,))] * 4 + [dma((sections,))] * 2 + [dma((sections - 1,))] * 2
        + [dma((sections,))] * 2 + [dma((sections - 1,))] * 2,
        compiler_params=pltpu.CompilerParams(
            collective_id=0, has_side_effects=True, vmem_limit_bytes=58 << 20),
        name="layer",
    )(decay_rates.T, reflect_betas.transpose(1, 2, 0), resets.reshape(1, tokens),
      queries, reflect_keys, reflect_values, out_weight, out_cotangent)
    return pl.pallas_call(
        results_kernel,
        in_specs=[hbm] * 3,
        out_specs=[hbm] * 2,
        out_shape=shapes,
        scratch_shapes=[pltpu.VMEM(a.shape, a.dtype) for a in parts] + [pltpu.VMEM(shapes[0].shape, BF16)]
        + [dma((PIECES + 2,)), dma((PIECES + 1,))],
        compiler_params=pltpu.CompilerParams(vmem_limit_bytes=58 << 20),
        name="results",
    )(own, cross, grads)


def solution(mesh):
    return jax.shard_map(
        per_device,
        mesh=mesh,
        in_specs=(
            P(("grp", "seq"), ("section", "head")),
            P(("grp", "seq"), None, ("section", "head")),
            P(("grp", "seq"), None, ("section", "head")),
            P(("grp", "seq"), None, ("section", "head")),
            P(("grp", "seq"), ("section", "head")),
            P(("grp", "seq")),
            P(("section", "head"), None),
            P(("grp", "seq"), ("section", "head")),
        ),
        out_specs=(
            P(("section", "head"), ("grp", "seq")),
            P(("grp", "seq"), None, ("section", "head")),
        ),
        check_vma=False,
    )
```

```python
import functools
import jax
import jax.numpy as jnp
from jax import lax
from jax.experimental import pallas as pl
from jax.experimental.pallas import tpu as pltpu
from jax.sharding import PartitionSpec as P

HALF = 64
BLK = 2 * HALF
F32 = jnp.float32
BF16 = jnp.bfloat16
NN = (((1,), (0,)), ((), ()))
NT = (((1,), (1,)), ((), ()))
TN = (((0,), (0,)), ((), ()))
MESH = pl.DeviceIdType.MESH


def dot1(a, b, dims=NN):
    return lax.dot_general(a.astype(BF16), b.astype(BF16), dims, preferred_element_type=F32)


def halves(a):
    high = a.astype(BF16)
    return high, (a - high.astype(F32)).astype(BF16)


def dot3(a, b, dims=NN):
    ah, al = halves(a)
    bh, bl = halves(b)
    n = b.shape[1]
    both = lax.dot_general(jnp.concatenate([ah, al], axis=1),
                           jnp.concatenate([jnp.concatenate([bh, bl], axis=1),
                                            jnp.concatenate([bh, jnp.zeros_like(bl)], axis=1)], axis=0),
                           dims, preferred_element_type=F32)
    return both[:, :n] + both[:, n:]


def thirds(a):
    top = a.astype(BF16)
    rest = a - top.astype(F32)
    middle = rest.astype(BF16)
    return jnp.concatenate([top, middle, (rest - middle.astype(F32)).astype(BF16)], axis=0)


def exact_dot(a, b):
    rows = a.shape[0]
    sums = dot1(thirds(a), b)
    return sums[:rows] + sums[rows:2 * rows] + sums[2 * rows:]


def iota(shape, axis):
    return lax.broadcasted_iota(jnp.int32, shape, axis)


def padded(parts, tokens):
    count = sum(p.shape[0] for p in parts)
    return jnp.concatenate(parts + [jnp.zeros((-count % 16, tokens), F32)], axis=0)


def schedules(decay, resets, betas):
    heads, tokens = decay.shape
    steps = 2 * tokens
    source, target = iota((tokens, 2 * tokens), 0), iota((tokens, 2 * tokens), 1)
    sums = exact_dot(padded([decay, resets], tokens), (source <= target) & (target < tokens)
                     | (source < target - tokens))
    inclusive, exclusive = sums[:, :tokens], sums[:, tokens:]
    even = padded([exclusive[:heads], inclusive[heads:heads + 1], betas[0]], tokens)
    odd = padded([inclusive[:heads + 1], betas[1]], tokens)
    source, target = iota((steps, steps), 0), iota((steps, steps), 1)
    spread = source == (target & 1) * tokens + (target >> 1)
    rows = exact_dot(jnp.concatenate([even, odd], axis=1), spread)

    def since_block(sums, size):
        edge = [jnp.zeros((heads + 1, size), F32)]
        for start in range(size, sums.shape[1], size):
            edge.append(jnp.broadcast_to(sums[:heads + 1, start - 1:start], (heads + 1, size)))
        edge = jnp.concatenate(edge, axis=1)
        kept = sums[heads:heads + 1] == edge[heads:]
        return jnp.where(kept, jnp.exp(jnp.where(kept, edge[:heads] - sums[:heads], 0.0)), 0.0)

    fades = since_block(rows, BLK) * rows[heads + 1:2 * heads + 1]
    cols = padded([rows[:2 * heads + 1], fades], steps).T
    tok_cols = padded([inclusive[:heads + 1], since_block(inclusive, HALF)], tokens).T
    return rows, cols, tok_cols


def local(heads, schedule, q_ref, k_refs, v_refs, yq_ref, yk_ref, r_ref, m_ref, o_ref, b_ref):
    rows, cols, tok_cols = schedule
    tokens = q_ref.shape[0]
    width = m_ref.shape[1]
    blocks = tokens // HALF
    steps = 2 * tokens
    everything = [(h, b) for h in range(heads) for b in range(blocks)]
    z_row, z_col, z_tok = rows[heads:heads + 1], cols[:, heads:heads + 1], tok_cols[:, heads:heads + 1]
    c_row = [rows[h:h + 1] for h in range(heads)]
    c_col = [cols[:, h:h + 1] for h in range(heads)]
    c_tok = [tok_cols[:, h:h + 1] for h in range(heads)]
    beta_row = [rows[heads + 1 + h:heads + 2 + h] for h in range(heads)]
    beta_col = [cols[:, heads + 1 + h:heads + 2 + h] for h in range(heads)]
    fade_col = [cols[:, 2 * heads + 1 + h:2 * heads + 2 + h] for h in range(heads)]
    fade_tok = [tok_cols[:, heads + 1 + h:heads + 2 + h] for h in range(heads)]
    z_end = z_row[:, steps - 1:]

    def sl(b):
        return slice(b * BLK, (b + 1) * BLK)

    def ts(b):
        return slice(b * HALF, (b + 1) * HALF)

    def lanes(h):
        return slice(h * width, (h + 1) * width)

    keys = {(h, b): k_refs[h][sl(b), :] for h, b in everything}
    tm_r, tm_c = iota((BLK, BLK), 0), iota((BLK, BLK), 1)
    eye = tm_r == tm_c
    identity = jnp.where(eye, 1.0, 0.0)

    low, scale_row, scale_col, gram = {}, {}, {}, {}

    def reach(h, b, c):
        edge = slice(b * BLK - 1, b * BLK)
        kept = z_row[:, sl(c)] == z_row[:, edge]
        gap = jnp.where(kept, c_row[h][:, sl(c)] - c_row[h][:, edge], 0.0)
        return jnp.where(kept, jnp.exp(gap) * scale_row[h, c], 0.0)

    for h, b in everything:
        for c in range(b + 1):
            gram[h, b, c] = dot1(keys[h, b], keys[h, c], NT)
    for h, b in everything:
        diag = jnp.where(eye, gram[h, b, b], 0.0)
        scale_row[h, b] = lax.rsqrt(jnp.sum(diag, axis=0, keepdims=True) + 1e-6)
        scale_col[h, b] = lax.rsqrt(jnp.sum(diag, axis=1, keepdims=True) + 1e-6)
    for h, b in everything:
        faded = fade_col[h][sl(b)] * scale_col[h, b]
        for c in range(b):
            low[h, b, c] = gram[h, b, c] * faded * reach(h, b, c)
        left = beta_col[h][sl(b)] * scale_col[h, b]
        valid = (z_col[sl(b)] == z_row[:, sl(b)]) & (tm_r > tm_c)
        gap = jnp.where(valid, c_row[h][:, sl(b)] - c_col[h][sl(b)], 0.0)
        low[h, b, b] = jnp.where(valid, jnp.exp(gap) * gram[h, b, b] * left * scale_row[h, b], 0.0)

    side = BLK // 2
    left = iota((side, BLK), 1) < side
    same = (tm_r >= side) == (tm_c >= side)
    row, col = iota((side, BLK), 0), iota((side, BLK), 1) & (side - 1)

    def narrowed(a):
        return jnp.where(left, a[:side], a[side:])

    def widened(a):
        return jnp.where(same, jnp.concatenate([a, a], axis=0), 0.0).astype(BF16)

    rounded = {i: low[i[0], i[1], i[1]].astype(BF16) for i in everything}
    small = {i: narrowed(low[i[0], i[1], i[1]]) for i in everything}
    inverse = {i: jnp.where(row == col, 1.0, 0.0) - jnp.where((row >> 1) == (col >> 1), small[i], 0.0)
               for i in everything}
    level = 2
    while (1 << level) <= side:
        pick = ((row >> level) == (col >> level)) & ((row >> (level - 1)) != (col >> (level - 1)))
        inner = {i: dot1(jnp.where(pick, small[i], 0.0), widened(inverse[i])) for i in everything}
        inverse = {i: inverse[i] - dot1(inverse[i], widened(inner[i])) for i in everything}
        level += 1
    inverse = {i: jnp.where(same, jnp.concatenate([inverse[i], inverse[i]], axis=0), 0.0) for i in everything}
    narrow = {i: inverse[i].astype(BF16) for i in everything}
    inner = {i: dot1(jnp.where(same, jnp.zeros_like(rounded[i]), rounded[i]), narrow[i]) for i in everything}
    inverse = {i: inverse[i] - dot1(narrow[i], inner[i]) for i in everything}
    for _ in range(2):
        residual = {i: dot3(low[i[0], i[1], i[1]], inverse[i]) + (inverse[i] - identity)
                    for i in everything}
        inverse = {i: inverse[i] - dot1(inverse[i], residual[i]) for i in everything}
    gamma_row = [jnp.where(z_row == 0, jnp.exp(-c_row[h]), 0.0) for h in range(heads)]

    def solve(hs, right):
        solved = {}
        for b in reversed(range(blocks)):
            for h in hs:
                x = right(h, b)
                if b + 1 < blocks:
                    later = []
                    for c in range(b + 1, blocks):
                        short = x.shape[0] - solved[h, c].shape[0]
                        later.append(jnp.concatenate([jnp.zeros((short, BLK), F32), solved[h, c]], axis=0)
                                     if short else solved[h, c])
                    x = x - dot3(jnp.concatenate(later, axis=1),
                                 jnp.concatenate([low[h, c, b] for c in range(b + 1, blocks)], axis=0))
                solved[h, b] = dot3(x, inverse[h, b])
        return solved

    def products(h, solved, y_ref):
        plain, moved = [], []
        for b in range(blocks):
            y = solved[h, b] * beta_row[h][:, sl(b)]
            short = y_ref.shape[1] - y.shape[0]
            if short:
                y = jnp.concatenate([jnp.zeros((short, BLK), F32), y], axis=0)
            plain.append(y.astype(BF16))
            moved.append((y * (gamma_row[h][:, sl(b)] * scale_row[h, b])).astype(BF16))
            y_ref[h, :, sl(b)] = plain[b]
        return (dot1(jnp.concatenate(plain, axis=1), v_refs[h][...]),
                dot1(jnp.concatenate(moved, axis=1), k_refs[h][...]))

    gamma_end_row = [jnp.where(z_row == z_end, jnp.exp(c_row[h] - c_row[h][:, steps - 1:]), 0.0)
                     for h in range(heads)]

    def end_side(h, b):
        return keys[h, b].astype(F32).T * (scale_row[h, b] * gamma_end_row[h][:, sl(b)])

    def token_side(h, b):
        parts = []
        for a in range(b, blocks):
            product = dot1(q_ref[ts(a), lanes(h)], keys[h, b], NT)
            if a > b:
                parts.append(product * fade_tok[h][ts(a)] * reach(h, a, b))
                continue
            valid = z_tok[ts(a)] == z_row[:, sl(b)]
            valid = valid & (iota((HALF, BLK), 0) >= (iota((HALF, BLK), 1) >> 1))
            gap = jnp.where(valid, c_row[h][:, sl(b)] - c_tok[h][ts(a)], 0.0)
            parts.append(jnp.where(valid, jnp.exp(gap) * product * scale_row[h, b], 0.0))
        return jnp.concatenate(parts, axis=0)

    def end_of(hs):
        solved = solve(hs, end_side)
        for h in hs:
            plain, moved = products(h, solved, yk_ref)
            gamma_end = jnp.where(z_end == 0, jnp.exp(-c_row[h][:, steps - 1:]), 0.0)
            b_ref[h] = plain
            m_ref[h] = jnp.where(iota((width, width), 0) == iota((width, width), 1), gamma_end, 0.0) - moved

    def tokens_of(hs):
        solved = solve(hs, token_side)
        for h in hs:
            plain, moved = products(h, solved, yq_ref)
            o_ref[h] = plain
            gamma_tok = jnp.where(z_tok == 0, jnp.exp(-c_tok[h]), 0.0)
            r_ref[h] = (gamma_tok * q_ref[:, lanes(h)].astype(F32) - moved).astype(BF16)

    return end_of, tokens_of


def layer_kernel(devices, sections, decay_ref, beta_ref, reset_ref, q_hbm, k_hbm, v_hbm, w_hbm, cot_hbm,
                 own_hbm, cross_in, g_hbm,
                 q_ref, k_ref, v_ref, w_ref, cot_ref, m_ref, mt_ref, b_ref, r_ref, o_ref, yq_ref, yk_ref, g_ref,
                 s_in, s_out, ds_in, ds_out, d, up_,
                 mixed, own, pair_out, pair_in, far_out, far_in, cross_out,
                 k_loaded, v_loaded, loaded, stored,
                 s_sent, s_got, ds_sent, ds_got, pair_sent, pair_got, cross_sent, cross_got,
                 near_sent, near_got, far_sent, far_got):
    heads, tokens, width = r_ref.shape
    features = own.shape[1]
    share = cot_hbm.shape[1]
    place = lax.axis_index("seq")
    section, core = lax.axis_index("section"), lax.axis_index("head")
    sibling = 1 - core
    first, last = place == 0, place == devices - 1

    def peer(k):
        return lax.rem(section + k, sections)

    def owned(part, side):
        return pl.ds(pl.multiple_of((part * 2 + side) * share, 128), share)

    barrier = pltpu.get_barrier_semaphore()

    @pl.when(jnp.logical_not(first))
    def _():
        pl.semaphore_signal(barrier, inc=1, device_id={"seq": place - 1}, device_id_type=MESH)

    @pl.when(jnp.logical_not(last))
    def _():
        pl.semaphore_signal(barrier, inc=1, device_id={"seq": place + 1}, device_id_type=MESH)

    pl.semaphore_signal(barrier, inc=1, device_id={"head": sibling}, device_id_type=MESH)
    for k in range(1, sections):
        pl.semaphore_signal(barrier, inc=1, device_id={"section": peer(k)}, device_id_type=MESH)

    def strip(h):
        return pl.ds(h * width, width)

    k_loads = [pltpu.make_async_copy(k_hbm.at[:, :, strip(h)], k_ref.at[h], k_loaded.at[h]) for h in range(heads)]
    v_loads = [pltpu.make_async_copy(v_hbm.at[:, :, strip(h)], v_ref.at[h], v_loaded.at[h]) for h in range(heads)]
    q_load = pltpu.make_async_copy(q_hbm, q_ref, loaded.at[0])
    w_load = pltpu.make_async_copy(w_hbm, w_ref, loaded.at[1])
    cot_load = pltpu.make_async_copy(cot_hbm, cot_ref.at[:, owned(section, core)], loaded.at[2])
    for load in k_loads + v_loads + [q_load, cot_load, w_load]:
        load.start()

    def far(k):
        return pltpu.make_async_remote_copy(
            src_ref=cot_hbm, dst_ref=cot_ref.at[:, owned(section, core)],
            send_sem=far_sent.at[k - 1], recv_sem=far_got.at[k - 1],
            device_id={"section": peer(k)}, device_id_type=MESH)

    def near(k):
        block = owned(peer(sections - k), core)
        return pltpu.make_async_remote_copy(
            src_ref=cot_ref.at[:, block] if k else cot_hbm, dst_ref=cot_ref.at[:, block],
            send_sem=near_sent.at[k], recv_sem=near_got.at[k],
            device_id={"head": sibling}, device_id_type=MESH)

    schedule = schedules(decay_ref[...], reset_ref[...].astype(F32), beta_ref[...])
    pl.semaphore_wait(barrier, sections + jnp.where(first, 0, 1) + jnp.where(last, 0, 1))
    for k in range(1, sections):
        far(k).start()
    near(0).start()
    k_refs = [k_ref.at[h].reshape(2 * tokens, width) for h in range(heads)]
    v_refs = [v_ref.at[h].reshape(2 * tokens, width) for h in range(heads)]

    def up(h):
        return pltpu.make_async_remote_copy(
            src_ref=s_out.at[h], dst_ref=s_in.at[h], send_sem=s_sent.at[h], recv_sem=s_got.at[h],
            device_id={"seq": place + 1}, device_id_type=MESH)

    def down(h):
        return pltpu.make_async_remote_copy(
            src_ref=ds_out.at[h], dst_ref=ds_in.at[h], send_sem=ds_sent.at[h], recv_sem=ds_got.at[h],
            device_id={"seq": place - 1}, device_id_type=MESH)

    def forward():
        for h in range(heads):
            up(h).wait_recv()

            @pl.when(jnp.logical_not(last))
            def _():
                s = s_in[h]
                mh, ml = halves(m_ref[h])
                s_out[h] = (dot1(mh, s) + dot1(ml, s) + b_ref[h]).astype(BF16)
                up(h).start()

    def backward():
        @pl.when(jnp.logical_not(first))
        def _():
            for h in range(heads):
                down(h).wait_recv()
                ds = ds_in[h]
                ds_out[h] = (dot1(mt_ref[h], jnp.concatenate([ds, ds], axis=0)) + d[h]).astype(BF16)
                down(h).start()

    def relay():
        for k in range(1, sections):
            far(k).wait_recv()
            near(k).start()

    for load in k_loads:
        load.wait()
    end_of, tokens_of = local(heads, schedule, q_ref, k_refs, v_refs, yq_ref, yk_ref, r_ref, m_ref, o_ref, b_ref)
    for load in v_loads + [q_load]:
        load.wait()

    parts = [range(heads // 2), range(heads // 2, heads)]
    for hs in [range(heads)]:
        @pl.when(jnp.logical_not(last))
        def _():
            end_of(hs)

        @pl.when(first)
        def _():
            for h in hs:
                s_in[h] = jnp.zeros(s_in.shape[1:], BF16)
                s_out[h] = b_ref[h].astype(BF16)
                up(h).start()

    tokens_of(parts[0])
    relay()

    @pl.when(place == 1)
    def _():
        forward()

    @pl.when(jnp.logical_not(last))
    def _():
        for h in range(heads):
            mt_ref[h] = jnp.concatenate(halves(m_ref[h].T), axis=1)

    tokens_of(parts[1])
    w_load.wait()
    cot_load.wait()
    for k in range(sections):
        near(k).wait_recv()
    up_[...] = dot1(cot_ref[...], w_ref[...], NT).astype(BF16)
    for h in range(heads):
        d[h] = dot1(r_ref[h], up_[:, strip(h)], TN)
    high, middle = 2 * place > devices, 2 * place == devices

    @pl.when(last)
    def _():
        for h in range(heads):
            ds_out[h] = d[h].astype(BF16)
            down(h).start()

    @pl.when(jnp.logical_and(high, jnp.logical_not(last)))
    def _():
        backward()

    @pl.when(place > 1)
    def _():
        forward()

    @pl.when(middle)
    def _():
        backward()

    for h in range(heads):
        mixed[:, strip(h)] = (dot1(r_ref[h], s_in[h]) + o_ref[h]).astype(BF16)

    def partial(target, side):
        start = pl.multiple_of((target * 2 + side) * features, 128)
        return dot1(mixed[...], w_ref[:, pl.ds(start, features)])

    def pair(k):
        return pltpu.make_async_remote_copy(
            src_ref=far_out.at[k - 1] if k else pair_out, dst_ref=far_in.at[k - 1] if k else pair_in, send_sem=pair_sent.at[k],
            recv_sem=pair_got.at[k], device_id={"head": sibling}, device_id_type=MESH)

    def cross(k):
        return pltpu.make_async_remote_copy(
            src_ref=cross_out.at[k - 1], dst_ref=cross_in.at[k - 1], send_sem=cross_sent.at[k - 1],
            recv_sem=cross_got.at[k - 1], device_id={"section": peer(k)}, device_id_type=MESH)

    for k in range(1, sections):
        far_out[k - 1] = partial(peer(k), sibling).astype(BF16)
        pair(k).start()
    for k in range(1, sections):
        mine = partial(peer(k), core)
        pair(k).wait_recv()
        cross_out[k - 1] = (mine + far_in[k - 1].astype(F32)).astype(BF16)
        cross(k).start()
    pair_out[...] = partial(section, sibling)
    pair(0).start()

    def g_store(h):
        return pltpu.make_async_copy(g_ref.at[h], g_hbm.at[:, :, strip(h)], stored.at[h])

    g_refs = [g_ref.at[h].reshape(2 * tokens, width) for h in range(heads)]
    for h in range(heads):
        g_refs[h][...] = dot1(yq_ref[h], up_[:, strip(h)], TN)
    total = partial(section, core)
    pair(0).wait_recv()
    own[...] = total + pair_in[...]
    own_store = pltpu.make_async_copy(own, own_hbm, stored.at[heads])
    own_store.start()

    @pl.when(2 * place < devices)
    def _():
        backward()

    for h in range(heads):
        @pl.when(first)
        def _():
            down(h).wait_recv()

        @pl.when(jnp.logical_not(last))
        def _():
            g_refs[h][...] += dot1(yk_ref[h], ds_in[h], TN)

        g_store(h).start()
    for k in range(1, sections):
        cross(k).wait_recv()
    for k in range(sections):
        pair(k).wait_send()
        near(k).wait_send()
    for k in range(1, sections):
        cross(k).wait_send()
        far(k).wait_send()

    @pl.when(jnp.logical_not(last))
    def _():
        for h in range(heads):
            up(h).wait_send()

    @pl.when(jnp.logical_not(first))
    def _():
        for h in range(heads):
            down(h).wait_send()

    for h in range(heads):
        g_store(h).wait()
    own_store.wait()


def results_kernel(own_hbm, cross_hbm, g_hbm, out_hbm, grads_hbm, own, cross, g, out, loaded, stored):
    pieces = loaded.shape[0] - 2
    rows = g.shape[0] // pieces
    parts = [pl.ds(i * rows, rows) for i in range(pieces)]
    loads = [pltpu.make_async_copy(own_hbm, own, loaded.at[0]), pltpu.make_async_copy(cross_hbm, cross, loaded.at[1])]
    loads += [pltpu.make_async_copy(g_hbm.at[p], g.at[p], loaded.at[2 + i]) for i, p in enumerate(parts)]
    stores = [pltpu.make_async_copy(out, out_hbm, stored.at[0])]
    stores += [pltpu.make_async_copy(g.at[p], grads_hbm.at[p], stored.at[1 + i]) for i, p in enumerate(parts)]
    for load in loads:
        load.start()
    loads[0].wait()
    loads[1].wait()
    total = own[...]
    for k in range(cross.shape[0]):
        total = total + cross[k].astype(F32)
    out[...] = total.T.astype(BF16)
    stores[0].start()
    for load, store in zip(loads[2:], stores[1:]):
        load.wait()
        store.start()
    for store in stores:
        store.wait()


PIECES = 4


def per_device(queries, reflect_keys, reflect_values, reflect_betas, decay_rates, resets,
               out_weight, out_cotangent):
    tokens = queries.shape[0]
    heads = reflect_betas.shape[2]
    width = queries.shape[1] // heads
    steps = 2 * tokens
    devices = lax.axis_size("seq")
    sections = lax.axis_size("section")
    features = out_weight.shape[1] // (2 * sections)

    square = (heads, width, width)
    pairs = (heads, tokens, 2, width)
    vmem = pl.BlockSpec(memory_space=pltpu.VMEM)
    hbm = pl.BlockSpec(memory_space=pl.ANY)
    dma = pltpu.SemaphoreType.DMA
    shapes = [jax.ShapeDtypeStruct((features, tokens), BF16),
              jax.ShapeDtypeStruct((tokens, 2, heads * width), F32)]
    parts = [jax.ShapeDtypeStruct((tokens, features), F32),
             jax.ShapeDtypeStruct((sections - 1, tokens, features), BF16), shapes[1]]
    own, cross, grads = pl.pallas_call(
        functools.partial(layer_kernel, devices, sections),
        in_specs=[vmem] * 3 + [hbm] * 5,
        out_specs=[hbm] * 3,
        out_shape=parts,
        scratch_shapes=[pltpu.VMEM(queries.shape, BF16), pltpu.VMEM(pairs, BF16), pltpu.VMEM(pairs, BF16),
                        pltpu.VMEM(out_weight.shape, BF16), pltpu.VMEM((tokens, out_weight.shape[1]), BF16),
                        pltpu.VMEM(square, F32), pltpu.VMEM((heads, width, 2 * width), BF16),
                        pltpu.VMEM(square, F32), pltpu.VMEM((heads, tokens, width), BF16), pltpu.VMEM((heads, tokens, width), F32),
                        pltpu.VMEM((heads, tokens, steps), BF16), pltpu.VMEM((heads, width, steps), BF16),
                        pltpu.VMEM(pairs, F32)]
        + [pltpu.VMEM(square, BF16)] * 4
        + [pltpu.VMEM(square, F32), pltpu.VMEM((tokens, heads * width), BF16)]
        + [pltpu.VMEM((tokens, heads * width), BF16), pltpu.VMEM((tokens, features), F32),
           pltpu.VMEM((tokens, features), F32), pltpu.VMEM((tokens, features), F32),
           pltpu.VMEM((sections - 1, tokens, features), BF16),
           pltpu.VMEM((sections - 1, tokens, features), BF16),
           pltpu.VMEM((sections - 1, tokens, features), BF16)]
        + [dma((heads,)), dma((heads,)), dma((3,)), dma((heads + 1,))]
        + [dma((heads,))] * 4 + [dma((sections,))] * 2 + [dma((sections - 1,))] * 2
        + [dma((sections,))] * 2 + [dma((sections - 1,))] * 2,
        compiler_params=pltpu.CompilerParams(
            collective_id=0, has_side_effects=True, vmem_limit_bytes=58 << 20),
        name="layer",
    )(decay_rates.T, reflect_betas.transpose(1, 2, 0), resets.reshape(1, tokens),
      queries, reflect_keys, reflect_values, out_weight, out_cotangent)
    return pl.pallas_call(
        results_kernel,
        in_specs=[hbm] * 3,
        out_specs=[hbm] * 2,
        out_shape=shapes,
        scratch_shapes=[pltpu.VMEM(a.shape, a.dtype) for a in parts] + [pltpu.VMEM(shapes[0].shape, BF16)]
        + [dma((PIECES + 2,)), dma((PIECES + 1,))],
        compiler_params=pltpu.CompilerParams(vmem_limit_bytes=58 << 20),
        name="results",
    )(own, cross, grads)


def solution(mesh):
    return jax.shard_map(
        per_device,
        mesh=mesh,
        in_specs=(
            P(("grp", "seq"), ("section", "head")),
            P(("grp", "seq"), None, ("section", "head")),
            P(("grp", "seq"), None, ("section", "head")),
            P(("grp", "seq"), None, ("section", "head")),
            P(("grp", "seq"), ("section", "head")),
            P(("grp", "seq")),
            P(("section", "head"), None),
            P(("grp", "seq"), ("section", "head")),
        ),
        out_specs=(
            P(("section", "head"), ("grp", "seq")),
            P(("grp", "seq"), None, ("section", "head")),
        ),
        check_vma=False,
    )
```

```python
import functools
import jax
import jax.numpy as jnp
from jax import lax
from jax.experimental import pallas as pl
from jax.experimental.pallas import tpu as pltpu
from jax.sharding import PartitionSpec as P

HALF = 64
BLK = 2 * HALF
F32 = jnp.float32
BF16 = jnp.bfloat16
NN = (((1,), (0,)), ((), ()))
NT = (((1,), (1,)), ((), ()))
TN = (((0,), (0,)), ((), ()))
MESH = pl.DeviceIdType.MESH


def dot1(a, b, dims=NN):
    return lax.dot_general(a.astype(BF16), b.astype(BF16), dims, preferred_element_type=F32)


def halves(a):
    high = a.astype(BF16)
    return high, (a - high.astype(F32)).astype(BF16)


def dot3(a, b, dims=NN):
    ah, al = halves(a)
    bh, bl = halves(b)
    n = b.shape[1]
    both = lax.dot_general(jnp.concatenate([ah, al], axis=1),
                           jnp.concatenate([jnp.concatenate([bh, bl], axis=1),
                                            jnp.concatenate([bh, jnp.zeros_like(bl)], axis=1)], axis=0),
                           dims, preferred_element_type=F32)
    return both[:, :n] + both[:, n:]


def thirds(a):
    top = a.astype(BF16)
    rest = a - top.astype(F32)
    middle = rest.astype(BF16)
    return jnp.concatenate([top, middle, (rest - middle.astype(F32)).astype(BF16)], axis=0)


def exact_dot(a, b):
    rows = a.shape[0]
    sums = dot1(thirds(a), b)
    return sums[:rows] + sums[rows:2 * rows] + sums[2 * rows:]


def iota(shape, axis):
    return lax.broadcasted_iota(jnp.int32, shape, axis)


def padded(parts, tokens):
    count = sum(p.shape[0] for p in parts)
    return jnp.concatenate(parts + [jnp.zeros((-count % 16, tokens), F32)], axis=0)


def schedules(decay, resets, betas):
    heads, tokens = decay.shape
    steps = 2 * tokens
    source, target = iota((tokens, 2 * tokens), 0), iota((tokens, 2 * tokens), 1)
    sums = exact_dot(padded([decay, resets], tokens), (source <= target) & (target < tokens)
                     | (source < target - tokens))
    inclusive, exclusive = sums[:, :tokens], sums[:, tokens:]
    even = padded([exclusive[:heads], inclusive[heads:heads + 1], betas[0]], tokens)
    odd = padded([inclusive[:heads + 1], betas[1]], tokens)
    source, target = iota((steps, steps), 0), iota((steps, steps), 1)
    spread = source == (target & 1) * tokens + (target >> 1)
    rows = exact_dot(jnp.concatenate([even, odd], axis=1), spread)

    def since_block(sums, size):
        edge = [jnp.zeros((heads + 1, size), F32)]
        for start in range(size, sums.shape[1], size):
            edge.append(jnp.broadcast_to(sums[:heads + 1, start - 1:start], (heads + 1, size)))
        edge = jnp.concatenate(edge, axis=1)
        kept = sums[heads:heads + 1] == edge[heads:]
        return jnp.where(kept, jnp.exp(jnp.where(kept, edge[:heads] - sums[:heads], 0.0)), 0.0)

    fades = since_block(rows, BLK) * rows[heads + 1:2 * heads + 1]
    cols = padded([rows[:2 * heads + 1], fades], steps).T
    tok_cols = padded([inclusive[:heads + 1], since_block(inclusive, HALF)], tokens).T
    return rows, cols, tok_cols


def local(heads, schedule, q_ref, k_refs, v_refs, yq_ref, yk_ref, r_ref, m_ref, o_ref, b_ref):
    rows, cols, tok_cols = schedule
    tokens = q_ref.shape[0]
    width = m_ref.shape[1]
    blocks = tokens // HALF
    steps = 2 * tokens
    everything = [(h, b) for h in range(heads) for b in range(blocks)]
    z_row, z_col, z_tok = rows[heads:heads + 1], cols[:, heads:heads + 1], tok_cols[:, heads:heads + 1]
    c_row = [rows[h:h + 1] for h in range(heads)]
    c_col = [cols[:, h:h + 1] for h in range(heads)]
    c_tok = [tok_cols[:, h:h + 1] for h in range(heads)]
    beta_row = [rows[heads + 1 + h:heads + 2 + h] for h in range(heads)]
    beta_col = [cols[:, heads + 1 + h:heads + 2 + h] for h in range(heads)]
    fade_col = [cols[:, 2 * heads + 1 + h:2 * heads + 2 + h] for h in range(heads)]
    fade_tok = [tok_cols[:, heads + 1 + h:heads + 2 + h] for h in range(heads)]
    z_end = z_row[:, steps - 1:]

    def sl(b):
        return slice(b * BLK, (b + 1) * BLK)

    def ts(b):
        return slice(b * HALF, (b + 1) * HALF)

    def lanes(h):
        return slice(h * width, (h + 1) * width)

    keys = {(h, b): k_refs[h][sl(b), :] for h, b in everything}
    tm_r, tm_c = iota((BLK, BLK), 0), iota((BLK, BLK), 1)
    eye = tm_r == tm_c
    identity = jnp.where(eye, 1.0, 0.0)

    low, scale_row, scale_col, gram = {}, {}, {}, {}

    def reach(h, b, c):
        edge = slice(b * BLK - 1, b * BLK)
        kept = z_row[:, sl(c)] == z_row[:, edge]
        gap = jnp.where(kept, c_row[h][:, sl(c)] - c_row[h][:, edge], 0.0)
        return jnp.where(kept, jnp.exp(gap) * scale_row[h, c], 0.0)

    for h, b in everything:
        for c in range(b + 1):
            gram[h, b, c] = dot1(keys[h, b], keys[h, c], NT)
    for h, b in everything:
        diag = jnp.where(eye, gram[h, b, b], 0.0)
        scale_row[h, b] = lax.rsqrt(jnp.sum(diag, axis=0, keepdims=True) + 1e-6)
        scale_col[h, b] = lax.rsqrt(jnp.sum(diag, axis=1, keepdims=True) + 1e-6)
    for h, b in everything:
        faded = fade_col[h][sl(b)] * scale_col[h, b]
        for c in range(b):
            low[h, b, c] = gram[h, b, c] * faded * reach(h, b, c)
        left = beta_col[h][sl(b)] * scale_col[h, b]
        valid = (z_col[sl(b)] == z_row[:, sl(b)]) & (tm_r > tm_c)
        gap = jnp.where(valid, c_row[h][:, sl(b)] - c_col[h][sl(b)], 0.0)
        low[h, b, b] = jnp.where(valid, jnp.exp(gap) * gram[h, b, b] * left * scale_row[h, b], 0.0)

    side = BLK // 2
    left = iota((side, BLK), 1) < side
    same = (tm_r >= side) == (tm_c >= side)
    row, col = iota((side, BLK), 0), iota((side, BLK), 1) & (side - 1)

    def narrowed(a):
        return jnp.where(left, a[:side], a[side:])

    def widened(a):
        return jnp.where(same, jnp.concatenate([a, a], axis=0), 0.0).astype(BF16)

    rounded = {i: low[i[0], i[1], i[1]].astype(BF16) for i in everything}
    small = {i: narrowed(low[i[0], i[1], i[1]]) for i in everything}
    inverse = {i: jnp.where(row == col, 1.0, 0.0) - jnp.where((row >> 1) == (col >> 1), small[i], 0.0)
               for i in everything}
    level = 2
    while (1 << level) <= side:
        pick = ((row >> level) == (col >> level)) & ((row >> (level - 1)) != (col >> (level - 1)))
        inner = {i: dot1(jnp.where(pick, small[i], 0.0), widened(inverse[i])) for i in everything}
        inverse = {i: inverse[i] - dot1(inverse[i], widened(inner[i])) for i in everything}
        level += 1
    inverse = {i: jnp.where(same, jnp.concatenate([inverse[i], inverse[i]], axis=0), 0.0) for i in everything}
    narrow = {i: inverse[i].astype(BF16) for i in everything}
    inner = {i: dot1(jnp.where(same, jnp.zeros_like(rounded[i]), rounded[i]), narrow[i]) for i in everything}
    inverse = {i: inverse[i] - dot1(narrow[i], inner[i]) for i in everything}
    for _ in range(2):
        residual = {i: dot3(low[i[0], i[1], i[1]], inverse[i]) + (inverse[i] - identity)
                    for i in everything}
        inverse = {i: inverse[i] - dot1(inverse[i], residual[i]) for i in everything}
    gamma_row = [jnp.where(z_row == 0, jnp.exp(-c_row[h]), 0.0) for h in range(heads)]

    def solve(hs, right):
        solved = {}
        for b in reversed(range(blocks)):
            for h in hs:
                x = right(h, b)
                if b + 1 < blocks:
                    later = []
                    for c in range(b + 1, blocks):
                        short = x.shape[0] - solved[h, c].shape[0]
                        later.append(jnp.concatenate([jnp.zeros((short, BLK), F32), solved[h, c]], axis=0)
                                     if short else solved[h, c])
                    x = x - dot3(jnp.concatenate(later, axis=1),
                                 jnp.concatenate([low[h, c, b] for c in range(b + 1, blocks)], axis=0))
                solved[h, b] = dot3(x, inverse[h, b])
        return solved

    def products(h, solved, y_ref):
        plain, moved = [], []
        for b in range(blocks):
            y = solved[h, b] * beta_row[h][:, sl(b)]
            short = y_ref.shape[1] - y.shape[0]
            if short:
                y = jnp.concatenate([jnp.zeros((short, BLK), F32), y], axis=0)
            plain.append(y.astype(BF16))
            moved.append((y * (gamma_row[h][:, sl(b)] * scale_row[h, b])).astype(BF16))
            y_ref[h, :, sl(b)] = plain[b]
        return (dot1(jnp.concatenate(plain, axis=1), v_refs[h][...]),
                dot1(jnp.concatenate(moved, axis=1), k_refs[h][...]))

    gamma_end_row = [jnp.where(z_row == z_end, jnp.exp(c_row[h] - c_row[h][:, steps - 1:]), 0.0)
                     for h in range(heads)]

    def end_side(h, b):
        return keys[h, b].astype(F32).T * (scale_row[h, b] * gamma_end_row[h][:, sl(b)])

    def token_side(h, b):
        parts = []
        column = dot1(q_ref[b * HALF:, lanes(h)], keys[h, b], NT)
        for a in range(b, blocks):
            product = column[ts(a - b)]
            if a > b:
                parts.append(product * fade_tok[h][ts(a)] * reach(h, a, b))
                continue
            valid = z_tok[ts(a)] == z_row[:, sl(b)]
            valid = valid & (iota((HALF, BLK), 0) >= (iota((HALF, BLK), 1) >> 1))
            gap = jnp.where(valid, c_row[h][:, sl(b)] - c_tok[h][ts(a)], 0.0)
            parts.append(jnp.where(valid, jnp.exp(gap) * product * scale_row[h, b], 0.0))
        return jnp.concatenate(parts, axis=0)

    def end_of(hs):
        solved = solve(hs, end_side)
        for h in hs:
            plain, moved = products(h, solved, yk_ref)
            gamma_end = jnp.where(z_end == 0, jnp.exp(-c_row[h][:, steps - 1:]), 0.0)
            b_ref[h] = plain
            m_ref[h] = jnp.where(iota((width, width), 0) == iota((width, width), 1), gamma_end, 0.0) - moved

    def tokens_of(hs):
        solved = solve(hs, token_side)
        for h in hs:
            plain, moved = products(h, solved, yq_ref)
            o_ref[h] = plain
            gamma_tok = jnp.where(z_tok == 0, jnp.exp(-c_tok[h]), 0.0)
            r_ref[h] = (gamma_tok * q_ref[:, lanes(h)].astype(F32) - moved).astype(BF16)

    return end_of, tokens_of


def layer_kernel(devices, sections, decay_ref, beta_ref, reset_ref, q_hbm, k_hbm, v_hbm, w_hbm, cot_hbm,
                 own_hbm, cross_in, g_hbm,
                 q_ref, k_ref, v_ref, w_ref, cot_ref, m_ref, mt_ref, b_ref, r_ref, o_ref, yq_ref, yk_ref, g_ref,
                 s_in, s_out, ds_in, ds_out, d, up_,
                 mixed, own, pair_out, pair_in, far_out, far_in, cross_out,
                 k_loaded, v_loaded, loaded, stored,
                 s_sent, s_got, ds_sent, ds_got, pair_sent, pair_got, cross_sent, cross_got,
                 near_sent, near_got, far_sent, far_got):
    heads, tokens, width = r_ref.shape
    features = own.shape[1]
    share = cot_hbm.shape[1]
    place = lax.axis_index("seq")
    section, core = lax.axis_index("section"), lax.axis_index("head")
    sibling = 1 - core
    first, last = place == 0, place == devices - 1

    def peer(k):
        return lax.rem(section + k, sections)

    def owned(part, side):
        return pl.ds(pl.multiple_of((part * 2 + side) * share, 128), share)

    barrier = pltpu.get_barrier_semaphore()

    @pl.when(jnp.logical_not(first))
    def _():
        pl.semaphore_signal(barrier, inc=1, device_id={"seq": place - 1}, device_id_type=MESH)

    @pl.when(jnp.logical_not(last))
    def _():
        pl.semaphore_signal(barrier, inc=1, device_id={"seq": place + 1}, device_id_type=MESH)

    pl.semaphore_signal(barrier, inc=1, device_id={"head": sibling}, device_id_type=MESH)
    for k in range(1, sections):
        pl.semaphore_signal(barrier, inc=1, device_id={"section": peer(k)}, device_id_type=MESH)

    def strip(h):
        return pl.ds(h * width, width)

    k_loads = [pltpu.make_async_copy(k_hbm.at[:, :, strip(h)], k_ref.at[h], k_loaded.at[h]) for h in range(heads)]
    v_loads = [pltpu.make_async_copy(v_hbm.at[:, :, strip(h)], v_ref.at[h], v_loaded.at[h]) for h in range(heads)]
    q_load = pltpu.make_async_copy(q_hbm, q_ref, loaded.at[0])
    w_load = pltpu.make_async_copy(w_hbm, w_ref, loaded.at[1])
    cot_load = pltpu.make_async_copy(cot_hbm, cot_ref.at[:, owned(section, core)], loaded.at[2])
    for load in k_loads + v_loads + [q_load, cot_load, w_load]:
        load.start()

    def far(k):
        return pltpu.make_async_remote_copy(
            src_ref=cot_hbm, dst_ref=cot_ref.at[:, owned(section, core)],
            send_sem=far_sent.at[k - 1], recv_sem=far_got.at[k - 1],
            device_id={"section": peer(k)}, device_id_type=MESH)

    def near(k):
        block = owned(peer(sections - k), core)
        return pltpu.make_async_remote_copy(
            src_ref=cot_ref.at[:, block] if k else cot_hbm, dst_ref=cot_ref.at[:, block],
            send_sem=near_sent.at[k], recv_sem=near_got.at[k],
            device_id={"head": sibling}, device_id_type=MESH)

    schedule = schedules(decay_ref[...], reset_ref[...].astype(F32), beta_ref[...])
    pl.semaphore_wait(barrier, sections + jnp.where(first, 0, 1) + jnp.where(last, 0, 1))
    for k in range(1, sections):
        far(k).start()
    near(0).start()
    k_refs = [k_ref.at[h].reshape(2 * tokens, width) for h in range(heads)]
    v_refs = [v_ref.at[h].reshape(2 * tokens, width) for h in range(heads)]

    def up(h):
        return pltpu.make_async_remote_copy(
            src_ref=s_out.at[h], dst_ref=s_in.at[h], send_sem=s_sent.at[h], recv_sem=s_got.at[h],
            device_id={"seq": place + 1}, device_id_type=MESH)

    def down(h):
        return pltpu.make_async_remote_copy(
            src_ref=ds_out.at[h], dst_ref=ds_in.at[h], send_sem=ds_sent.at[h], recv_sem=ds_got.at[h],
            device_id={"seq": place - 1}, device_id_type=MESH)

    def forward():
        for h in range(heads):
            up(h).wait_recv()

            @pl.when(jnp.logical_not(last))
            def _():
                s = s_in[h]
                mh, ml = halves(m_ref[h])
                s_out[h] = (dot1(mh, s) + dot1(ml, s) + b_ref[h]).astype(BF16)
                up(h).start()

    def backward():
        @pl.when(jnp.logical_not(first))
        def _():
            for h in range(heads):
                down(h).wait_recv()
                ds = ds_in[h]
                ds_out[h] = (dot1(mt_ref[h], jnp.concatenate([ds, ds], axis=0)) + d[h]).astype(BF16)
                down(h).start()

    def relay():
        for k in range(1, sections):
            far(k).wait_recv()
            near(k).start()

    for load in k_loads:
        load.wait()
    end_of, tokens_of = local(heads, schedule, q_ref, k_refs, v_refs, yq_ref, yk_ref, r_ref, m_ref, o_ref, b_ref)
    for load in v_loads + [q_load]:
        load.wait()

    parts = [range(heads // 2), range(heads // 2, heads)]
    for hs in [range(heads)]:
        @pl.when(jnp.logical_not(last))
        def _():
            end_of(hs)

        @pl.when(first)
        def _():
            for h in hs:
                s_in[h] = jnp.zeros(s_in.shape[1:], BF16)
                s_out[h] = b_ref[h].astype(BF16)
                up(h).start()

    tokens_of(parts[0])
    relay()

    @pl.when(place == 1)
    def _():
        forward()

    @pl.when(jnp.logical_not(last))
    def _():
        for h in range(heads):
            mt_ref[h] = jnp.concatenate(halves(m_ref[h].T), axis=1)

    tokens_of(parts[1])
    w_load.wait()
    cot_load.wait()
    for k in range(sections):
        near(k).wait_recv()
    up_[...] = dot1(cot_ref[...], w_ref[...], NT).astype(BF16)
    for h in range(heads):
        d[h] = dot1(r_ref[h], up_[:, strip(h)], TN)
    high, middle = 2 * place > devices, 2 * place == devices

    @pl.when(last)
    def _():
        for h in range(heads):
            ds_out[h] = d[h].astype(BF16)
            down(h).start()

    @pl.when(jnp.logical_and(high, jnp.logical_not(last)))
    def _():
        backward()

    @pl.when(place > 1)
    def _():
        forward()

    @pl.when(middle)
    def _():
        backward()

    for h in range(heads):
        mixed[:, strip(h)] = (dot1(r_ref[h], s_in[h]) + o_ref[h]).astype(BF16)

    def partial(target, side):
        start = pl.multiple_of((target * 2 + side) * features, 128)
        return dot1(mixed[...], w_ref[:, pl.ds(start, features)])

    def pair(k):
        return pltpu.make_async_remote_copy(
            src_ref=far_out.at[k - 1] if k else pair_out, dst_ref=far_in.at[k - 1] if k else pair_in, send_sem=pair_sent.at[k],
            recv_sem=pair_got.at[k], device_id={"head": sibling}, device_id_type=MESH)

    def cross(k):
        return pltpu.make_async_remote_copy(
            src_ref=cross_out.at[k - 1], dst_ref=cross_in.at[k - 1], send_sem=cross_sent.at[k - 1],
            recv_sem=cross_got.at[k - 1], device_id={"section": peer(k)}, device_id_type=MESH)

    for k in range(1, sections):
        far_out[k - 1] = partial(peer(k), sibling).astype(BF16)
        pair(k).start()
    for k in range(1, sections):
        mine = partial(peer(k), core)
        pair(k).wait_recv()
        cross_out[k - 1] = (mine + far_in[k - 1].astype(F32)).astype(BF16)
        cross(k).start()
    pair_out[...] = partial(section, sibling)
    pair(0).start()

    def g_store(h):
        return pltpu.make_async_copy(g_ref.at[h], g_hbm.at[:, :, strip(h)], stored.at[h])

    g_refs = [g_ref.at[h].reshape(2 * tokens, width) for h in range(heads)]
    for h in range(heads):
        g_refs[h][...] = dot1(yq_ref[h], up_[:, strip(h)], TN)
    total = partial(section, core)
    pair(0).wait_recv()
    own[...] = total + pair_in[...]
    own_store = pltpu.make_async_copy(own, own_hbm, stored.at[heads])
    own_store.start()

    @pl.when(2 * place < devices)
    def _():
        backward()

    for h in range(heads):
        @pl.when(first)
        def _():
            down(h).wait_recv()

        @pl.when(jnp.logical_not(last))
        def _():
            g_refs[h][...] += dot1(yk_ref[h], ds_in[h], TN)

        g_store(h).start()
    for k in range(1, sections):
        cross(k).wait_recv()
    for k in range(sections):
        pair(k).wait_send()
        near(k).wait_send()
    for k in range(1, sections):
        cross(k).wait_send()
        far(k).wait_send()

    @pl.when(jnp.logical_not(last))
    def _():
        for h in range(heads):
            up(h).wait_send()

    @pl.when(jnp.logical_not(first))
    def _():
        for h in range(heads):
            down(h).wait_send()

    for h in range(heads):
        g_store(h).wait()
    own_store.wait()


def results_kernel(own_hbm, cross_hbm, g_hbm, out_hbm, grads_hbm, own, cross, g, out, loaded, stored):
    pieces = loaded.shape[0] - 2
    rows = g.shape[0] // pieces
    parts = [pl.ds(i * rows, rows) for i in range(pieces)]
    loads = [pltpu.make_async_copy(own_hbm, own, loaded.at[0]), pltpu.make_async_copy(cross_hbm, cross, loaded.at[1])]
    loads += [pltpu.make_async_copy(g_hbm.at[p], g.at[p], loaded.at[2 + i]) for i, p in enumerate(parts)]
    stores = [pltpu.make_async_copy(out, out_hbm, stored.at[0])]
    stores += [pltpu.make_async_copy(g.at[p], grads_hbm.at[p], stored.at[1 + i]) for i, p in enumerate(parts)]
    for load in loads:
        load.start()
    loads[0].wait()
    loads[1].wait()
    total = own[...]
    for k in range(cross.shape[0]):
        total = total + cross[k].astype(F32)
    out[...] = total.T.astype(BF16)
    stores[0].start()
    for load, store in zip(loads[2:], stores[1:]):
        load.wait()
        store.start()
    for store in stores:
        store.wait()


PIECES = 4


def per_device(queries, reflect_keys, reflect_values, reflect_betas, decay_rates, resets,
               out_weight, out_cotangent):
    tokens = queries.shape[0]
    heads = reflect_betas.shape[2]
    width = queries.shape[1] // heads
    steps = 2 * tokens
    devices = lax.axis_size("seq")
    sections = lax.axis_size("section")
    features = out_weight.shape[1] // (2 * sections)

    square = (heads, width, width)
    pairs = (heads, tokens, 2, width)
    vmem = pl.BlockSpec(memory_space=pltpu.VMEM)
    hbm = pl.BlockSpec(memory_space=pl.ANY)
    dma = pltpu.SemaphoreType.DMA
    shapes = [jax.ShapeDtypeStruct((features, tokens), BF16),
              jax.ShapeDtypeStruct((tokens, 2, heads * width), F32)]
    parts = [jax.ShapeDtypeStruct((tokens, features), F32),
             jax.ShapeDtypeStruct((sections - 1, tokens, features), BF16), shapes[1]]
    own, cross, grads = pl.pallas_call(
        functools.partial(layer_kernel, devices, sections),
        in_specs=[vmem] * 3 + [hbm] * 5,
        out_specs=[hbm] * 3,
        out_shape=parts,
        scratch_shapes=[pltpu.VMEM(queries.shape, BF16), pltpu.VMEM(pairs, BF16), pltpu.VMEM(pairs, BF16),
                        pltpu.VMEM(out_weight.shape, BF16), pltpu.VMEM((tokens, out_weight.shape[1]), BF16),
                        pltpu.VMEM(square, F32), pltpu.VMEM((heads, width, 2 * width), BF16),
                        pltpu.VMEM(square, F32), pltpu.VMEM((heads, tokens, width), BF16), pltpu.VMEM((heads, tokens, width), F32),
                        pltpu.VMEM((heads, tokens, steps), BF16), pltpu.VMEM((heads, width, steps), BF16),
                        pltpu.VMEM(pairs, F32)]
        + [pltpu.VMEM(square, BF16)] * 4
        + [pltpu.VMEM(square, F32), pltpu.VMEM((tokens, heads * width), BF16)]
        + [pltpu.VMEM((tokens, heads * width), BF16), pltpu.VMEM((tokens, features), F32),
           pltpu.VMEM((tokens, features), F32), pltpu.VMEM((tokens, features), F32),
           pltpu.VMEM((sections - 1, tokens, features), BF16),
           pltpu.VMEM((sections - 1, tokens, features), BF16),
           pltpu.VMEM((sections - 1, tokens, features), BF16)]
        + [dma((heads,)), dma((heads,)), dma((3,)), dma((heads + 1,))]
        + [dma((heads,))] * 4 + [dma((sections,))] * 2 + [dma((sections - 1,))] * 2
        + [dma((sections,))] * 2 + [dma((sections - 1,))] * 2,
        compiler_params=pltpu.CompilerParams(
            collective_id=0, has_side_effects=True, vmem_limit_bytes=58 << 20),
        name="layer",
    )(decay_rates.T, reflect_betas.transpose(1, 2, 0), resets.reshape(1, tokens),
      queries, reflect_keys, reflect_values, out_weight, out_cotangent)
    return pl.pallas_call(
        results_kernel,
        in_specs=[hbm] * 3,
        out_specs=[hbm] * 2,
        out_shape=shapes,
        scratch_shapes=[pltpu.VMEM(a.shape, a.dtype) for a in parts] + [pltpu.VMEM(shapes[0].shape, BF16)]
        + [dma((PIECES + 2,)), dma((PIECES + 1,))],
        compiler_params=pltpu.CompilerParams(vmem_limit_bytes=58 << 20),
        name="results",
    )(own, cross, grads)


def solution(mesh):
    return jax.shard_map(
        per_device,
        mesh=mesh,
        in_specs=(
            P(("grp", "seq"), ("section", "head")),
            P(("grp", "seq"), None, ("section", "head")),
            P(("grp", "seq"), None, ("section", "head")),
            P(("grp", "seq"), None, ("section", "head")),
            P(("grp", "seq"), ("section", "head")),
            P(("grp", "seq")),
            P(("section", "head"), None),
            P(("grp", "seq"), ("section", "head")),
        ),
        out_specs=(
            P(("section", "head"), ("grp", "seq")),
            P(("grp", "seq"), None, ("section", "head")),
        ),
        check_vma=False,
    )
```
